32 devices in a mesh: slab: 8 (over z, x), sub: 4 (over y, core).
Axes of the slice: x: 2, y: 2, z: 4, core: 2. Of those that a mesh axis runs over, the one named last changes fastest.
Arguments:
- state: float32 [9, 56, 2048], P(None, None, ('slab', 'sub')), may hold values from -6 to 6
- star: float32 [3, 9, 9, 2048], P(None, None, None, ('slab', 'sub')), may hold values from -2 to 2
- aminus: float32 [4, 9, 9, 2048], P(None, None, None, ('slab', 'sub')), may hold values from -1 to 1
- aplus: float32 [4, 9, 9, 2048], P(None, None, None, ('slab', 'sub')), may hold values from -1 to 1
- ck_stiff: float32 [3, 56, 56], replicated, may hold values from -0.75 to 0.75
- vol_stiff: float32 [3, 56, 56], replicated, may hold values from -0.75 to 0.75
- flux_local: float32 [4, 56, 56], replicated, may hold values from -0.75 to 0.75
- lift: float32 [4, 56, 21], replicated, may hold values from -1.25 to 1.25
- rotate: float32 [3, 21, 21], replicated, may hold values from -1.25 to 1.25
- project: float32 [4, 21, 56], replicated, may hold values from -0.75 to 0.75
- cluster: int32 [2048], P(('slab', 'sub')), may hold values from 0 to 2, as said below
- orient: int32 [4, 2048], P(None, ('slab', 'sub')), may hold values from 0 to 2
- neighbour: int32 [4, 2048], P(None, ('slab', 'sub')), may hold values from 0 to 383, as said below
- send_elem: int32 [4, 1024], P(None, ('slab', 'sub')), may hold values from 0 to 63
- send_face: int32 [4, 1024], P(None, ('slab', 'sub')), may hold values from 0 to 3
Outputs:
- new_state: float32 [9, 56, 2048], P(None, None, ('slab', 'sub'))
The draws below stay inside these ranges and needn't reach their ends.
Inputs may be any that keep to these rules, and one draw needn't show every extreme that they name: cluster 0, 1, 2 means 1, 2, 4 steps in the coarsest step. `neighbour`: an entry x below 256 names face x // 64 of local element x % 64; otherwise x - 256 = d * 32 + s names slot s of direction d. An element of cluster 2 names only slots below 8, of cluster 1 only slots from 8 below 16, of cluster 0 only slots from 16.
All inputs are finite; a program needn't handle non-finite values.
Results may differ from the reference program's by a relative error of at most 0.0003.
Values sent between devices are 32-bit elements; how exact they have to be, the bound alone decides.
No kernel may reach another device: no remote copies, remote signals or barrier semaphores. Data moves between devices by JAX's collectives and lax.ppermute only.
A program may use at most 64 MiB of HBM per device.

```python
import jax
import jax.numpy as jnp
from jax import lax

FIELDS = 9
MODES = 56
FACE_MODES = 21
DERIVS = 6
TICKS = 4
ELEM_DEV = 64
SLOT_FINE = 8
SLOT_COARSE = 16
BORDER_SLOTS = 32
ELEMS = 2048
SLOTS_ALL = 1024
N_SLAB = 8
N_SUB = 4


def links_draw(key):
    base = jax.random.fold_in(key, 7)
    keys = jax.random.split(base, 5)
    groups = jax.random.randint(keys[0], (ELEMS,), 0, 3)
    groups = groups.at[0].set(0)
    remote = jax.random.randint(keys[1], (4, ELEMS), 0, 4) == 0
    inside = jax.random.randint(keys[2], (4, ELEMS), 0, 4 * ELEM_DEV)
    direction = jax.random.randint(keys[3], (4, ELEMS), 0, 4)
    width = jnp.where(groups == 0, SLOT_COARSE, SLOT_FINE)
    first = jnp.where(groups == 2, 0, jnp.where(groups == 1, SLOT_FINE, 2 * SLOT_FINE))
    upper = jnp.broadcast_to(width[None, :], (4, ELEMS))
    slot = first[None, :] + jax.random.randint(keys[4], (4, ELEMS), 0, upper)
    far = 4 * ELEM_DEV + direction * BORDER_SLOTS + slot
    links = jnp.where(remote, far, inside)
    links = links.at[3, 0].set(4 * ELEM_DEV + 4 * BORDER_SLOTS - 1)
    links = links.at[0, 0].set(0)
    return (groups.astype(jnp.int32), links.astype(jnp.int32))


def draw_cluster(key, part):
    return links_draw(key)[0]


def draw_neighbour(key, part):
    return links_draw(key)[1]


def with_ends(values, key, low, largest):
    dims = values.shape
    place = [jax.random.randint(jax.random.fold_in(key, axis), (), 0, dims[axis]) for axis in range(len(dims))]
    values = values.at[tuple(place)].set(low)
    longest = dims.index(max(dims))
    place[longest] = (place[longest] + 1) % dims[longest]
    return values.at[tuple(place)].set(largest)


def steps_of(rng, shape, pieces, low, high):
    def one(axis_at, shards_of):
        draws = jax.random.uniform(jax.random.fold_in(jax.random.fold_in(rng, 6), axis_at), (shards_of,), jnp.float32, low / len(pieces), high / len(pieces))
        return jnp.repeat(jnp.exp(draws), shape[axis_at] // shards_of).reshape((-1,) + (1,) * (len(shape) - axis_at - 1))

    gain = one(*pieces[0])
    for cut in pieces[1:]:
        gain = gain * one(*cut)
    return gain


def gaussian(own_key, extent, deviation, bound, pieces=(), held_as=jnp.bfloat16):
    drawn = deviation * jax.random.normal(own_key, extent, jnp.float32)
    if pieces:
        drawn = drawn * steps_of(own_key, extent, pieces, -0.22, 0.18)
    return jnp.clip(drawn, -bound, bound).astype(held_as)


def setup_inputs(seed: int = 0) -> dict:
    key_of = jax.random.split(jax.random.key(seed), 16)
    return {
        "state": gaussian(key_of[0], (FIELDS, MODES, ELEMS), 1.0, 6.0, ((2, 32),), jnp.float32),
        "star": gaussian(key_of[1], (3, FIELDS, FIELDS, ELEMS), FIELDS ** -0.5, 2.0, ((3, 32),), jnp.float32),
        "aminus": gaussian(key_of[2], (4, FIELDS, FIELDS, ELEMS), (4 * FIELDS) ** -0.5, 1.0, ((3, 32),), jnp.float32),
        "aplus": gaussian(key_of[3], (4, FIELDS, FIELDS, ELEMS), (4 * FIELDS) ** -0.5, 1.0, ((3, 32),), jnp.float32),
        "ck_stiff": gaussian(key_of[4], (3, MODES, MODES), MODES ** -0.5, 0.75, (), jnp.float32),
        "vol_stiff": gaussian(key_of[5], (3, MODES, MODES), MODES ** -0.5, 0.75, (), jnp.float32),
        "flux_local": gaussian(key_of[6], (4, MODES, MODES), MODES ** -0.5, 0.75, (), jnp.float32),
        "lift": gaussian(key_of[7], (4, MODES, FACE_MODES), FACE_MODES ** -0.5, 1.25, (), jnp.float32),
        "rotate": gaussian(key_of[8], (3, FACE_MODES, FACE_MODES), FACE_MODES ** -0.5, 1.25, (), jnp.float32),
        "project": gaussian(key_of[9], (4, FACE_MODES, MODES), MODES ** -0.5, 0.75, (), jnp.float32),
        "cluster": draw_cluster(jax.random.fold_in(key_of[15], 71), 0),
        "orient": with_ends(jax.random.randint(key_of[11], (4, ELEMS), 0, 3), jax.random.fold_in(key_of[11], 1), 0, 2).astype(jnp.int32),
        "neighbour": draw_neighbour(jax.random.fold_in(key_of[15], 71), 0),
        "send_elem": with_ends(jax.random.randint(key_of[13], (4, SLOTS_ALL), 0, ELEM_DEV), jax.random.fold_in(key_of[13], 1), 0, ELEM_DEV - 1).astype(jnp.int32),
        "send_face": with_ends(jax.random.randint(key_of[14], (4, SLOTS_ALL), 0, 4), jax.random.fold_in(key_of[14], 1), 0, 3).astype(jnp.int32),
    }


TOP_LEVEL = lax.Precision.HIGHEST
TIME_STEP = 1.0


def taylor_weights(offset):
    width = TIME_STEP / 4.0
    start = offset.astype(jnp.float32)
    rows = []
    factorial = 1.0
    for order in range(DERIVS):
        factorial = factorial * (order + 1)
        rows.append(((start + 1.0) ** (order + 1) - start ** (order + 1)) * (width ** (order + 1) / factorial))
    return jnp.stack(rows)


def predict(start, star, ck_stiff):
    terms = [start]
    for order in range(DERIVS - 1):
        moved = jnp.einsum('dmn,fne->dfme', ck_stiff, terms[-1], precision=TOP_LEVEL)
        terms.append(-jnp.einsum('dfge,dfme->gme', star, moved, precision=TOP_LEVEL))
    return jnp.stack(terms)


def face_values(field_values, project):
    elems = field_values.shape[-1]
    lookup_table = jnp.einsum('dnk,tkv->tndv', project, field_values, precision=TOP_LEVEL)
    return lookup_table.reshape(FIELDS, FACE_MODES, 4 * elems)


def apply_update(state, own, lookup_table, lookup, turned, finished, star, aminus, aplus, vol_stiff, flux_local, lift, rotate):
    volume = jnp.einsum('dfge,dfme->gme', star, jnp.einsum('dmn,fne->dfme', vol_stiff, own, precision=TOP_LEVEL), precision=TOP_LEVEL)
    inner = jnp.einsum('jfge,jfme->gme', aminus, jnp.einsum('jmn,fne->jfme', flux_local, own, precision=TOP_LEVEL), precision=TOP_LEVEL)
    outer_values = jnp.take(lookup_table, lookup, axis=2)
    aligned = jnp.einsum('opq,fqje,oje->fpje', rotate, outer_values, turned, precision=TOP_LEVEL)
    lifted = jnp.einsum('jmp,fpje->jfme', lift, aligned, precision=TOP_LEVEL)
    outer = jnp.einsum('jfge,jfme->gme', aplus, lifted, precision=TOP_LEVEL)
    return jnp.where(finished[None, None], state + volume - inner - outer, state)


def reference(state, star, aminus, aplus, ck_stiff, vol_stiff, flux_local, lift, rotate, project, cluster, orient, neighbour, send_elem, send_face):
    devices = N_SLAB * N_SUB
    fine = SLOT_FINE

    def split(array):
        array = array.reshape(array.shape[:-1] + (devices, array.shape[-1] // devices))
        array = jnp.moveaxis(array, -2, 0)
        return array.reshape((N_SLAB, N_SUB) + array.shape[1:])

    def merge(array):
        array = array.reshape((devices,) + array.shape[2:])
        array = jnp.moveaxis(array, 0, -2)
        return array.reshape(array.shape[:-2] + (array.shape[-2] * array.shape[-1],))

    def over_devices(func, field_values):
        return lax.map(lambda row: jax.vmap(func)(*row), field_values)

    local_state = split(state)
    local_star = split(star)
    local_minus = split(aminus)
    local_plus = split(aplus)
    local_cluster = split(cluster)
    local_orient = split(orient)
    local_neighbour = split(neighbour)
    local_elem = split(send_elem)
    local_face = split(send_face)

    start_state = local_state
    two_sum = jnp.zeros_like(local_state)
    four_sum = jnp.zeros_like(local_state)
    coarse_two = None
    coarse_four = None
    current = local_state
    for tick in range(TICKS):
        def phase_one(now, begun, two_prev, four_prev, groups, elem_star, element_listing, face_list):
            elems = now.shape[-1]
            period = jnp.where(groups == 0, 4, jnp.where(groups == 1, 2, 1))
            offset = tick % period
            begun = jnp.where((offset == 0)[None, None], now, begun)
            derivs = predict(begun, elem_star, ck_stiff)
            integral = jnp.einsum('ke,kfme->fme', taylor_weights(offset), derivs, precision=TOP_LEVEL)
            two_new = integral if tick % 2 == 0 else two_prev + integral
            four_new = integral if tick == 0 else four_prev + integral
            table_one = face_values(integral, project)
            outgoing = jnp.take(table_one, face_list * elems + element_listing, axis=2)
            return begun, integral, two_new, four_new, outgoing

        start_state, integral, two_sum, four_sum, outgoing = over_devices(
            phase_one, (current, start_state, two_sum, four_sum, local_cluster, local_star, local_elem, local_face))
        arrived = jnp.stack([
            jnp.roll(outgoing[:, :, :, :, 0], 1, axis=0),
            jnp.roll(outgoing[:, :, :, :, 1], -1, axis=0),
            jnp.roll(outgoing[:, :, :, :, 2], 1, axis=1),
            jnp.roll(outgoing[:, :, :, :, 3], -1, axis=1)], axis=4)
        coarse_two = arrived[..., fine:2 * fine] if tick % 2 == 0 else coarse_two + arrived[..., fine:2 * fine]
        coarse_four = arrived[..., 2 * fine:] if tick == 0 else coarse_four + arrived[..., 2 * fine:]
        remote = jnp.concatenate([arrived[..., :fine], coarse_two, coarse_four], axis=5)

        def second_phase(now, integral_now, two_now, four_now, remote_now, groups, turns, links, elem_star, elem_minus, elem_plus):
            elems = now.shape[-1]
            slots = remote_now.shape[-1]
            period = jnp.where(groups == 0, 4, jnp.where(groups == 1, 2, 1))
            offset = tick % period
            window = jnp.where(groups == 2, 0, jnp.where(groups == 1, 1, 2))
            own = jnp.where((groups == 2)[None, None], integral_now, jnp.where((groups == 1)[None, None], two_now, four_now))
            table_one = face_values(integral_now, project)
            second_table = face_values(two_now, project) if tick % 2 == 1 else table_one
            table_four = face_values(four_now, project) if tick == 3 else table_one
            lookup_table = jnp.concatenate([table_one, second_table, table_four, remote_now.reshape(FIELDS, FACE_MODES, 4 * slots)], axis=2)
            lookup = jnp.where(links < 4 * elems, links + window[None, :] * (4 * elems), links + 8 * elems)
            turned = (turns[None] == jnp.arange(3)[:, None, None]).astype(jnp.float32)
            return apply_update(now, own, lookup_table, lookup, turned, offset == period - 1, elem_star, elem_minus, elem_plus, vol_stiff, flux_local, lift, rotate)

        current = over_devices(second_phase, (current, integral, two_sum, four_sum, remote, local_cluster, local_orient, local_neighbour, local_star, local_minus, local_plus))
    return merge(current)
```

```python
import functools

import jax
import jax.numpy as jnp
from jax import lax
from jax.experimental import pallas as pl
from jax.experimental.pallas import tpu as pltpu
from jax.sharding import PartitionSpec as P

FIELDS = 9
PAIRS = 5
MODES = 56
MODES_UP = 64
FACE_MODES = 21
FACE_UP = 24
ROWS = 2 * PAIRS * FACE_UP
DERIVS = 6
TICKS = 4
SLOT = 8
TIME_STEP = 1.0
F32 = jnp.float32
BF16 = jnp.bfloat16
BLOCKS = ((0, 32), (32, 24))


def from_behind(x, axis, by):
    size = lax.axis_size(axis)
    return lax.ppermute(x, axis, [(i, (i + by) % size) for i in range(size)])


def taylor_constants():
    width = TIME_STEP / TICKS
    table = []
    for begin in range(TICKS):
        factorial = 1.0
        row = []
        for order in range(DERIVS):
            factorial = factorial * (order + 1)
            span = float((begin + 1) ** (order + 1) - begin ** (order + 1))
            row.append(span * width ** (order + 1) / factorial)
        table.append(row)
    return table


def low_half(shape, half):
    return lax.broadcasted_iota(jnp.int32, shape, len(shape) - 1) < half


def swap(x, half):
    return pltpu.roll(x, half, x.ndim - 1)


def pair(a, b):
    return jnp.concatenate([a, b], axis=-1)


def halves(x):
    high = x.astype(BF16).astype(F32)
    return high, x - high


def pad_rows(x, rows):
    if x.shape[0] == rows:
        return x
    return jnp.concatenate([x, jnp.zeros((rows - x.shape[0], x.shape[1]), x.dtype)], axis=0)


def timing(cluster, tick):
    period = jnp.where(cluster == 0, 4, jnp.where(cluster == 1, 2, 1))
    offset = jnp.where(cluster == 0, tick % 4, jnp.where(cluster == 1, tick % 2, 0))
    return offset, offset == period - 1


def put_right(ref, start, values):
    rows = values.shape[0]
    up = -(-rows // 16) * 16
    high = pad_rows(values, up).astype(BF16)
    low = pad_rows(values - values.astype(BF16).astype(F32), up).astype(BF16)
    return high, low


def store_right(ref, row, col, values):
    high, low = put_right(ref, row, values)
    up = high.shape[0]
    width = values.shape[1]
    ref[row : row + up, col : col + width] = high
    ref[MODES_UP + row : MODES_UP + row + up, col : col + width] = high
    ref[2 * MODES_UP + row : 2 * MODES_UP + row + up, col : col + width] = low


def left_parts(matrix, up):
    rows = matrix.shape[0]
    high, low = halves(matrix)
    gap = jnp.zeros((rows, up - matrix.shape[1]), F32)
    return jnp.concatenate([high, gap, low, gap, high, gap], axis=1)


def contract(m_ref, coef_ref, dirs, lanes, emit):
    half = lanes // 2
    for row, count in BLOCKS:
        sums = [None] * FIELDS
        for d in range(dirs):
            for q in range(PAIRS):
                values = m_ref[d * MODES + row : d * MODES + row + count, q * lanes : (q + 1) * lanes]
                for g in range(FIELDS):
                    term = coef_ref[d * PAIRS + q, g : g + 1, :] * values
                    sums[g] = term if sums[g] is None else sums[g] + term
        low = low_half((count, lanes), half)
        for q in range(PAIRS):
            first = sums[2 * q]
            if 2 * q + 1 < FIELDS:
                second = sums[2 * q + 1]
                result = jnp.where(low, first, second) + swap(jnp.where(low, second, first), half)
            else:
                result = jnp.where(low, first + swap(first, half), 0.0)
            emit(row, count, q, result)


def predict(state_ref, ck_ref, star_ref, weight_ref, right_ref, m_ref, i_ref, lanes):
    for row, count in BLOCKS:
        for q in range(PAIRS):
            cols = slice(q * lanes, (q + 1) * lanes)
            values = state_ref[row : row + count, cols]
            i_ref[row : row + count, cols] = weight_ref[0:1, :] * values
            store_right(right_ref, row, q * lanes, values)

    def step(order, carry):
        m_ref[0 : 3 * MODES, :] = jnp.dot(ck_ref[...], right_ref[...], preferred_element_type=F32)
        weight = weight_ref[pl.ds(order + 1, 1), :]

        def emit(row, count, q, result):
            cols = slice(q * lanes, (q + 1) * lanes)
            i_ref[row : row + count, cols] += weight * result
            store_right(right_ref, row, q * lanes, result)

        contract(m_ref, star_ref, 3, lanes, emit)
        return carry

    lax.fori_loop(0, DERIVS - 1, step, 0)


def store_weights(weight_ref, cluster, tick):
    offset, _ = timing(cluster, tick)
    table = taylor_constants()
    for order in range(DERIVS):
        row = jnp.full(cluster.shape, table[0][order], F32)
        for begin in range(1, TICKS):
            row = jnp.where(offset == begin, table[begin][order], row)
        weight_ref[order : order + 1, :] = row


def project_faces(i_ref, proj_ref, right_ref, table_ref, lanes):
    half = lanes // 2
    for row, count in BLOCKS:
        for q in range(PAIRS):
            store_right(right_ref, row, q * lanes, i_ref[row : row + count, q * lanes : (q + 1) * lanes])
    faces = jnp.dot(proj_ref[...], right_ref[...], preferred_element_type=F32)
    low = low_half((FACE_UP, lanes), half)
    for q in range(PAIRS):
        for k in range(2):
            one = faces[2 * k * FACE_UP : (2 * k + 1) * FACE_UP, q * lanes : (q + 1) * lanes]
            two = faces[(2 * k + 1) * FACE_UP : (2 * k + 2) * FACE_UP, q * lanes : (q + 1) * lanes]
            crossed = swap(jnp.where(low, two, one), half)
            table_ref[2 * q * FACE_UP : (2 * q + 1) * FACE_UP, k * lanes : (k + 1) * lanes] = jnp.where(low, one, crossed)
            table_ref[(2 * q + 1) * FACE_UP : (2 * q + 2) * FACE_UP, k * lanes : (k + 1) * lanes] = jnp.where(
                low, crossed, two
            )


def pick(table, chosen):
    rows = table.shape[0]
    high, low = halves(table)
    both = jnp.concatenate([high, low], axis=0).astype(BF16)
    out = jnp.dot(both, chosen, preferred_element_type=F32)
    return out[:rows] + out[rows:]


def one_hot(index_row, rows, base=0):
    sub = lax.broadcasted_iota(jnp.int32, (rows, index_row.shape[1]), 0) + base
    return jnp.where(sub == index_row, 1.0, 0.0).astype(BF16)


def fill_messages(tables, send_index, out_refs, lanes):
    lane = lax.broadcasted_iota(jnp.int32, (FACE_UP, lanes), 1)
    column = lane // 32
    place = (lane // SLOT) % 4
    for group, table in enumerate(tables):
        elems4 = table.shape[1]
        chosen = one_hot(send_index[group : group + 1, :], elems4)
        picked = pick(table, chosen)
        quads = []
        for quad in range(3):
            merged = picked[4 * quad * FACE_UP : (4 * quad + 1) * FACE_UP]
            for c in range(1, 4):
                f = 4 * quad + c
                if f < FIELDS:
                    merged = jnp.where(column == c, picked[f * FACE_UP : (f + 1) * FACE_UP], merged)
            quads.append(merged)
        for d in range(4):
            message = None
            for quad in range(3):
                shift = ((quad - d) * SLOT) % lanes
                moved = quads[quad] if shift == 0 else pltpu.roll(quads[quad], shift, 1)
                message = moved if message is None else jnp.where(place == quad, moved, message)
            out_refs[d][group * FACE_UP : (group + 1) * FACE_UP, :] = message


def take_messages(in_refs, groups, far_ref, lanes):
    lane = lax.broadcasted_iota(jnp.int32, (FACE_UP, lanes), 1)
    column = lane // 32
    place = (lane // SLOT) % 4
    lefts = []
    for group in range(groups):
        arrived = [ref[group * FACE_UP : (group + 1) * FACE_UP, :] for ref in in_refs]
        pieces = []
        for quad in range(3):
            merged = None
            for d in range(4):
                shift = ((d - quad) * SLOT) % lanes
                moved = arrived[d] if shift == 0 else pltpu.roll(arrived[d], shift, 1)
                merged = moved if merged is None else jnp.where(place == d, moved, merged)
            for c in range(4):
                if 4 * quad + c < FIELDS:
                    pieces.append(jnp.where(column == c, merged, 0.0))
        pieces.append(jnp.zeros((FACE_UP, lanes), F32))
        lefts.append(jnp.concatenate(pieces, axis=0))
    left = lefts[0] if groups == 1 else jnp.concatenate(lefts, axis=1)
    return pick(left, far_ref[0 : groups * lanes, :])


def outer_update(in_refs, groups, near_ref, far_ref, aplus_ref, turn_ref, orient_ref, base_ref, cluster, tick, c_ref, out_ref, lanes):
    half = lanes // 2
    low = low_half((FACE_UP, lanes), half)
    values = near_ref[...] + take_messages(in_refs, groups, far_ref, lanes)
    zeros = jnp.zeros((SLOT, lanes), F32)
    for k in range(2):
        sums = [None] * FIELDS
        for f in range(FIELDS):
            part = values[f * FACE_UP : (f + 1) * FACE_UP, k * lanes : (k + 1) * lanes]
            for g in range(FIELDS):
                term = aplus_ref[k * FIELDS + f, g : g + 1, :] * part
                sums[g] = term if sums[g] is None else sums[g] + term
        for q in range(PAIRS):
            first = sums[2 * q]
            if 2 * q + 1 < FIELDS:
                second = sums[2 * q + 1]
                crossed = swap(jnp.where(low, second, first), half)
                sides = (jnp.where(low, first, crossed), jnp.where(low, crossed, second))
            else:
                crossed = swap(first, half)
                sides = (jnp.where(low, first, 0.0), jnp.where(low, crossed, 0.0))
            for side in range(2):
                high, rest = halves(sides[side])
                stacked = jnp.concatenate([high, high, rest, zeros], axis=0).astype(BF16)
                c_ref[2 * k + side, :, q * lanes : (q + 1) * lanes] = stacked
    _, finished = timing(cluster, tick)
    for j in range(4):
        turned = jnp.dot(turn_ref[j], c_ref[j], preferred_element_type=F32)
        which = orient_ref[j : j + 1, :]
        which = pair(which, which)
        for q in range(PAIRS):
            cols = slice(q * lanes, (q + 1) * lanes)
            term = jnp.where(
                which == 0,
                turned[0:MODES, cols],
                jnp.where(which == 1, turned[MODES : 2 * MODES, cols], turned[2 * MODES : 3 * MODES, cols]),
            )
            before = base_ref[:, cols] if j == 0 else out_ref[:, cols]
            out_ref[:, cols] = jnp.where(finished, before - term, before)


def pack_pairs(ref, axis_pairs, lead, out_ref):
    for a in range(lead):
        for q in range(axis_pairs):
            one = ref[a, 2 * q]
            two = ref[a, 2 * q + 1] if 2 * q + 1 < FIELDS else jnp.zeros_like(one)
            out_ref[a * axis_pairs + q] = pair(one, two)


def first_kernel(
    state_ref, star_ref, ck_ref, project_ref, cluster_ref, send_ref,
    m0, m1, m2, m3, packed_ref, star_out, ck_out, proj_out, i_ref, table_ref,
    right_ref, m_ref, weight_ref, *, lanes,
):
    for q in range(PAIRS):
        one = state_ref[2 * q]
        two = state_ref[2 * q + 1] if 2 * q + 1 < FIELDS else jnp.zeros_like(one)
        packed_ref[:, q * lanes : (q + 1) * lanes] = pair(one, two)
    pack_pairs(star_ref, PAIRS, 3, star_out)
    ck = -ck_ref[...].reshape(3 * MODES, MODES)
    ck_out[...] = left_parts(ck, MODES_UP).astype(BF16)
    proj_rows = [pad_rows(project_ref[j], FACE_UP) for j in range(4)]
    proj_out[...] = left_parts(jnp.concatenate(proj_rows, axis=0), MODES_UP).astype(BF16)
    cluster = pair(cluster_ref[...], cluster_ref[...])
    store_weights(weight_ref, cluster, 0)
    predict(packed_ref, ck_out, star_out, weight_ref, right_ref, m_ref, i_ref, lanes)
    project_faces(i_ref, proj_out, right_ref, table_ref, lanes)
    fill_messages([table_ref[...]], send_ref[...], (m0, m1, m2, m3), lanes)


def prepare_kernel(
    star_ref, aminus_ref, aplus_ref, vol_ref, flux_ref, lift_ref, rotate_ref, neighbour_ref,
    coef_out, aplus_out, left_out, turn_out, near_out, far_out, *, lanes,
):
    half = lanes // 2
    pack_pairs(star_ref, PAIRS, 3, coef_out)
    for a in range(4):
        for q in range(PAIRS):
            one = aminus_ref[a, 2 * q]
            two = aminus_ref[a, 2 * q + 1] if 2 * q + 1 < FIELDS else jnp.zeros_like(one)
            coef_out[(3 + a) * PAIRS + q] = pair(one, two)
    for k in range(2):
        for f in range(FIELDS):
            aplus_out[k * FIELDS + f] = pair(aplus_ref[2 * k, f], aplus_ref[2 * k + 1, f])
    left_out[0 : 3 * MODES, :] = left_parts(vol_ref[...].reshape(3 * MODES, MODES), MODES_UP)
    left_out[3 * MODES : 7 * MODES, :] = left_parts(-flux_ref[...].reshape(4 * MODES, MODES), MODES_UP)
    for j in range(4):
        for which in range(3):
            turned = jnp.dot(lift_ref[j], rotate_ref[which], precision=lax.Precision.HIGHEST, preferred_element_type=F32)
            parts = left_parts(turned, FACE_UP)
            gap = jnp.zeros((MODES, SLOT), F32)
            turn_out[j, which * MODES : (which + 1) * MODES, :] = jnp.concatenate([parts, gap], axis=1)
    row = jnp.concatenate([neighbour_ref[j : j + 1, :] for j in range(4)], axis=1)
    near_out[...] = one_hot(row, 4 * half)
    sub = lax.broadcasted_iota(jnp.int32, (lanes, 4 * half), 0)
    for group in range(4):
        target = 4 * half + ((sub // SLOT) % 4) * 32 + group * SLOT + sub % SLOT
        far_out[group * lanes : (group + 1) * lanes, :] = jnp.where(target == row, 1.0, 0.0).astype(BF16)


def local_kernel(
    i_ref, packed_ref, table_ref, cluster_ref, coef_ref, left_ref, near_ref, own_ref, seen_ref,
    base_out, own_out, seen_out, right_ref, m_ref, *, lanes, tick,
):
    cluster = pair(cluster_ref[...], cluster_ref[...])
    offset, finished = timing(cluster, tick)
    fresh = offset == 0
    for row, count in BLOCKS:
        for q in range(PAIRS):
            cols = slice(q * lanes, (q + 1) * lanes)
            values = i_ref[row : row + count, cols]
            if tick:
                values = jnp.where(fresh, values, own_ref[row : row + count, cols] + values)
            own_out[row : row + count, cols] = values
            store_right(right_ref, row, q * lanes, values)
    seen = pick(table_ref[...], near_ref[...])
    if tick:
        twice = pair(fresh, fresh) if False else jnp.concatenate([offset, offset], axis=1) == 0
        seen = jnp.where(twice, seen, seen_ref[...] + seen)
    seen_out[...] = seen
    m_ref[...] = jnp.dot(left_ref[...], right_ref[...], preferred_element_type=F32)

    def emit(row, count, q, result):
        cols = slice(q * lanes, (q + 1) * lanes)
        before = packed_ref[row : row + count, cols]
        base_out[row : row + count, cols] = jnp.where(finished, before + result, before)

    contract(m_ref, coef_ref, 7, lanes, emit)


def tick_kernel(
    r0, r1, r2, r3, near_ref, far_ref, aplus_ref, turn_ref, orient_ref, base_ref, cluster_ref,
    ck_ref, proj_ref, star_ref, send_ref, *rest, lanes, tick, olds, groups,
):
    old_refs = rest[:olds]
    m0, m1, m2, m3, packed_ref, i_ref, table_ref = rest[olds : olds + 7]
    rest = rest[olds + 7 :]
    sum_ref = None
    if tick == 1:
        sum_ref, rest = rest[0], rest[1:]
    right_ref, m_ref, weight_ref, c_ref = rest
    cluster = pair(cluster_ref[...], cluster_ref[...])
    outer_update(
        (r0, r1, r2, r3), groups, near_ref, far_ref, aplus_ref, turn_ref, orient_ref, base_ref,
        cluster, tick - 1, c_ref, packed_ref, lanes,
    )
    store_weights(weight_ref, cluster, tick)
    predict(packed_ref, ck_ref, star_ref, weight_ref, right_ref, m_ref, i_ref, lanes)
    project_faces(i_ref, proj_ref, right_ref, table_ref, lanes)
    table = table_ref[...]
    tables = [table]
    if tick == 1:
        two = old_refs[0][...] + table
        sum_ref[...] = two
        tables.append(two)
    if tick == 3:
        two = old_refs[0][...] + table
        four = old_refs[1][...] + two
        tables += [two, four, four]
    fill_messages(tables, send_ref[...], (m0, m1, m2, m3), lanes)


def last_kernel(
    r0, r1, r2, r3, near_ref, far_ref, aplus_ref, turn_ref, orient_ref, base_ref, cluster_ref,
    out_ref, packed_ref, c_ref, *, lanes,
):
    half = lanes // 2
    cluster = pair(cluster_ref[...], cluster_ref[...])
    outer_update(
        (r0, r1, r2, r3), 4, near_ref, far_ref, aplus_ref, turn_ref, orient_ref, base_ref,
        cluster, TICKS - 1, c_ref, packed_ref, lanes,
    )
    for f in range(FIELDS):
        begin = (f // 2) * lanes + (f % 2) * half
        out_ref[f] = packed_ref[:, begin : begin + half]


def call(body, outs, scratch, name, flops, arrays):
    moved = sum(a.size * a.dtype.itemsize for a in arrays)
    return pl.pallas_call(
        body,
        out_shape=outs,
        in_specs=[pl.BlockSpec(memory_space=pltpu.VMEM)] * len(arrays),
        out_specs=[pl.BlockSpec(memory_space=pltpu.VMEM)] * len(outs),
        scratch_shapes=scratch,
        compiler_params=pltpu.CompilerParams(vmem_limit_bytes=24 << 20),
        cost_estimate=pl.CostEstimate(flops=flops, bytes_accessed=moved, transcendentals=0),
        name=name,
    )(*arrays)


def shards(
    state, star, aminus, aplus, ck_stiff, vol_stiff, flux_local, lift, rotate, project,
    cluster, orient, neighbour, send_elem, send_face,
):
    elems = state.shape[-1]
    lanes = 2 * elems
    wide = PAIRS * lanes
    shape = jax.ShapeDtypeStruct
    cluster_row = cluster.reshape(1, elems)
    slots = send_elem.shape[1]
    groups = slots // SLOT
    send = (send_face * elems + send_elem).reshape(4, groups, SLOT)
    send = jnp.tile(jnp.transpose(send, (1, 0, 2)).reshape(groups, 4 * SLOT), (1, lanes // (4 * SLOT)))

    modal = shape((MODES, wide), F32)
    table = shape((ROWS, 4 * elems), F32)
    right = pltpu.VMEM((3 * MODES_UP, wide), BF16)
    weights = pltpu.VMEM((SLOT, lanes), F32)
    faces = pltpu.VMEM((4, 80, wide), BF16)

    def message(count):
        return [shape((count * FACE_UP, lanes), F32)] * 4

    out = call(
        functools.partial(first_kernel, lanes=lanes),
        message(1)
        + [
            modal,
            shape((3 * PAIRS, FIELDS, lanes), F32),
            shape((3 * MODES, 3 * MODES_UP), BF16),
            shape((4 * FACE_UP, 3 * MODES_UP), BF16),
            modal,
            table,
        ],
        [right, pltpu.VMEM((3 * MODES, wide), F32), weights],
        "first", 400_000_000, (state, star, ck_stiff, project, cluster_row, send),
    )
    messages, (packed, star_pairs, ck_left, proj_left, integral, table_now) = out[:4], out[4:]
    coef, aplus_pairs, left, turn, near_hot, far_hot = call(
        functools.partial(prepare_kernel, lanes=lanes),
        [
            shape((7 * PAIRS, FIELDS, lanes), F32),
            shape((2 * FIELDS, FIELDS, lanes), F32),
            shape((7 * MODES, 3 * MODES_UP), F32),
            shape((4, 3 * MODES, 80), F32),
            shape((4 * elems, 4 * elems), BF16),
            shape((4 * lanes, 4 * elems), BF16),
        ],
        [],
        "prepare", 100_000_000,
        (star, aminus, aplus, vol_stiff, flux_local, lift, rotate, neighbour),
    )
    left = left.astype(BF16)
    turn = turn.astype(BF16)
    own = integral
    seen = table_now
    tables = []
    two = None
    for tick in range(TICKS):
        arrived = [
            from_behind(messages[0], "slab", 1),
            from_behind(messages[1], "slab", -1),
            from_behind(messages[2], "sub", 1),
            from_behind(messages[3], "sub", -1),
        ]
        base, own, seen = call(
            functools.partial(local_kernel, lanes=lanes, tick=tick),
            [modal, modal, table],
            [right, pltpu.VMEM((7 * MODES, wide), F32)],
            f"local{tick}", 300_000_000,
            (integral, packed, table_now, cluster_row, coef, left, near_hot, own, seen),
        )
        count = (1, 2, 1, 4)[tick]
        common = (*arrived, seen, far_hot, aplus_pairs, turn, orient, base, cluster_row)
        if tick == TICKS - 1:
            return call(
                functools.partial(last_kernel, lanes=lanes),
                [shape(state.shape, F32)],
                [pltpu.VMEM((MODES, wide), F32), faces],
                "last", 100_000_000, common,
            )[0]
        olds = {0: (table_now,), 1: (), 2: (table_now, two)}[tick]
        sends = (1, 2, 1, 4)[tick + 1]
        out = call(
            functools.partial(tick_kernel, lanes=lanes, tick=tick + 1, olds=len(olds), groups=count),
            message(sends) + [modal, modal, table] + ([table] if tick == 0 else []),
            [right, pltpu.VMEM((3 * MODES, wide), F32), weights, faces],
            f"tick{tick + 1}", 500_000_000,
            (*common, ck_left, proj_left, star_pairs, send, *olds),
        )
        messages, (packed, integral, table_now) = out[:4], out[4:7]
        if tick == 0:
            two = out[7]


def solution(mesh):
    placed = (
        P(None, None, ("slab", "sub")),
        P(None, None, None, ("slab", "sub")),
        P(None, None, None, ("slab", "sub")),
        P(None, None, None, ("slab", "sub")),
        P(),
        P(),
        P(),
        P(),
        P(),
        P(),
        P(("slab", "sub")),
        P(None, ("slab", "sub")),
        P(None, ("slab", "sub")),
        P(None, ("slab", "sub")),
        P(None, ("slab", "sub")),
    )
    return jax.shard_map(
        shards,
        mesh=mesh,
        in_specs=placed,
        out_specs=P(None, None, ("slab", "sub")),
        check_vma=False,
    )
```

```python
import functools

import jax
import jax.numpy as jnp
from jax import lax
from jax.experimental import pallas as pl
from jax.experimental.pallas import tpu as pltpu
from jax.sharding import PartitionSpec as P

FIELDS = 9
PAIRS = 5
MODES = 56
MODES_UP = 64
FACE_MODES = 21
FACE_UP = 24
ROWS = 2 * PAIRS * FACE_UP
DERIVS = 6
TICKS = 4
SLOT = 8
TIME_STEP = 1.0
F32 = jnp.float32
BF16 = jnp.bfloat16
BLOCKS = ((0, 32), (32, 24))
GROUPS = ((0, 1), (2, 3), (4,))


def paired(axis):
    return lax.axis_size(axis) % 2 == 0


def exchange(x, axis, phase):
    size = lax.axis_size(axis)
    if paired(axis):
        pairs = []
        for i in range(phase, size + phase, 2):
            one, two = i % size, (i + 1) % size
            pairs += [(one, two), (two, one)]
    else:
        by = 1 if phase == 0 else -1
        pairs = [(i, (i + by) % size) for i in range(size)]
    return lax.ppermute(x, axis, pairs)


def taylor_constants():
    width = TIME_STEP / TICKS
    table = []
    for begin in range(TICKS):
        factorial = 1.0
        row = []
        for order in range(DERIVS):
            factorial = factorial * (order + 1)
            span = float((begin + 1) ** (order + 1) - begin ** (order + 1))
            row.append(span * width ** (order + 1) / factorial)
        table.append(row)
    return table


def low_half(shape, half):
    return lax.broadcasted_iota(jnp.int32, shape, len(shape) - 1) < half


def swap(x, half):
    return pltpu.roll(x, half, x.ndim - 1)


def pair(a, b):
    return jnp.concatenate([a, b], axis=-1)


def halves(x):
    high = x.astype(BF16).astype(F32)
    return high, x - high


def pad_rows(x, rows):
    if x.shape[0] == rows:
        return x
    return jnp.concatenate([x, jnp.zeros((rows - x.shape[0], x.shape[1]), x.dtype)], axis=0)


def timing(cluster, tick):
    period = jnp.where(cluster == 0, 4, jnp.where(cluster == 1, 2, 1))
    offset = jnp.where(cluster == 0, tick % 4, jnp.where(cluster == 1, tick % 2, 0))
    return offset, offset == period - 1


def right_operand(values):
    values = pad_rows(values, MODES_UP)
    high = values.astype(BF16)
    low = (values - high.astype(F32)).astype(BF16)
    return jnp.concatenate([high, high, low], axis=0)


def left_parts(matrix, up):
    rows = matrix.shape[0]
    if up > matrix.shape[1]:
        matrix = jnp.concatenate([matrix, jnp.zeros((rows, up - matrix.shape[1]), F32)], axis=1)
    high, low = halves(matrix)
    return jnp.concatenate([high, low, high], axis=1)


def send_choice(even, forward, backward):
    return jnp.where(even, forward, backward), jnp.where(even, backward, forward)


def parity(axis):
    if not paired(axis):
        return True, False
    even = lax.rem(lax.axis_index(axis), 2) == 0
    return even, even


def products(m_ref, slot, left, values, dirs, group, lanes):
    out = jnp.dot(left, right_operand(values), preferred_element_type=F32)
    if group == GROUPS[-1]:
        low = low_half((MODES, lanes), lanes // 2)
        for i in range(0, dirs, 2):
            one = out[i * MODES : (i + 1) * MODES]
            if i + 1 < dirs:
                one = jnp.where(low, one, out[(i + 1) * MODES : (i + 2) * MODES])
            m_ref[slot, (i // 2) * MODES : (i // 2 + 1) * MODES, group[0] * lanes : (group[0] + 1) * lanes] = one
    else:
        m_ref[slot, 0 : dirs * MODES, group[0] * lanes : (group[-1] + 1) * lanes] = out


def contract(m_ref, slot, coef_ref, dirs, group, lanes):
    half = lanes // 2
    fields = [g for q in group for g in (2 * q, 2 * q + 1) if g < FIELDS]
    terms = [(d, q, q, d) for q in range(PAIRS - 1) for d in range(dirs)]
    terms += [(i, PAIRS - 1, PAIRS - 1, i) for i in range((dirs + 1) // 2)]
    columns = {q: [] for q in group}
    for row, count in BLOCKS:
        sums = {}
        for d, q, block, line in terms:
            values = m_ref[slot, d * MODES + row : d * MODES + row + count, q * lanes : (q + 1) * lanes]
            for g in fields:
                term = coef_ref[block * FIELDS + g, line : line + 1, :] * values
                sums[g] = sums[g] + term if g in sums else term
        low = low_half((count, lanes), half)
        for q in group:
            first = sums[2 * q]
            if 2 * q + 1 < FIELDS:
                second = sums[2 * q + 1]
                result = jnp.where(low, first, second) + swap(jnp.where(low, second, first), half)
            else:
                result = first + swap(first, half)
            columns[q].append(result)
    columns = [jnp.concatenate(columns[q], axis=0) for q in group]
    return columns[0] if len(columns) == 1 else jnp.concatenate(columns, axis=1)


def span(group, lanes):
    return slice(group[0] * lanes, (group[-1] + 1) * lanes)


def predict(state_of, ck_ref, star_ref, weight_ref, proj_ref, face_ref, m_ref, i_ref, lanes):
    def weight(order, group):
        row = weight_ref[order : order + 1, :]
        return row if len(group) == 1 else pair(row, row)

    for group in GROUPS:
        values = state_of(group)
        i_ref[:, span(group, lanes)] = weight(0, group) * values
        products(m_ref, 0, ck_ref[...], values, 3, group, lanes)
    for order in range(1, DERIVS):
        for group in GROUPS:
            values = contract(m_ref, (order - 1) % 2, star_ref, 3, group, lanes)
            total = i_ref[:, span(group, lanes)] + weight(order, group) * values
            i_ref[:, span(group, lanes)] = total
            if order < DERIVS - 1:
                products(m_ref, order % 2, ck_ref[...], values, 3, group, lanes)
            else:
                face_ref[:, span(group, lanes)] = jnp.dot(
                    proj_ref[...], right_operand(total), preferred_element_type=F32
                )


def store_weights(weight_ref, cluster, tick):
    offset, _ = timing(cluster, tick)
    table = taylor_constants()
    for order in range(DERIVS):
        row = jnp.full(cluster.shape, table[0][order], F32)
        for begin in range(1, TICKS):
            row = jnp.where(offset == begin, table[begin][order], row)
        weight_ref[order : order + 1, :] = row


def fill_table(face_ref, table_ref, lanes):
    half = lanes // 2
    low = low_half((FACE_UP, lanes), half)
    for q in range(PAIRS):
        for k in range(2):
            one = face_ref[2 * k * FACE_UP : (2 * k + 1) * FACE_UP, q * lanes : (q + 1) * lanes]
            two = face_ref[(2 * k + 1) * FACE_UP : (2 * k + 2) * FACE_UP, q * lanes : (q + 1) * lanes]
            crossed = swap(jnp.where(low, two, one), half)
            table_ref[2 * q * FACE_UP : (2 * q + 1) * FACE_UP, k * lanes : (k + 1) * lanes] = jnp.where(low, one, crossed)
            table_ref[(2 * q + 1) * FACE_UP : (2 * q + 2) * FACE_UP, k * lanes : (k + 1) * lanes] = jnp.where(
                low, crossed, two
            )


def pick(table, chosen):
    rows = table.shape[0]
    high, low = halves(table)
    both = jnp.concatenate([high, low], axis=0).astype(BF16)
    out = jnp.dot(both, chosen, preferred_element_type=F32)
    return out[:rows] + out[rows:]


def one_hot(index_row, rows):
    sub = lax.broadcasted_iota(jnp.int32, (rows, index_row.shape[1]), 0)
    return jnp.where(sub == index_row, 1.0, 0.0).astype(BF16)


def lane_places(rows, lanes):
    lane = lax.broadcasted_iota(jnp.int32, (rows, lanes), 1)
    return lane // (4 * SLOT), (lane // SLOT) % 4


def send_rows(face_ref, elem_ref, lanes):
    slots = face_ref.shape[1]
    half = lanes // 2
    index = face_ref[...] * half + elem_ref[...]
    index = jnp.concatenate([index] * (lanes // slots), axis=1)
    _, place = lane_places(1, lanes)
    rows = []
    for group in range(slots // SLOT):
        row = None
        for d in range(4):
            shift = ((d - group) * SLOT) % lanes
            moved = index[d : d + 1, :]
            moved = pltpu.roll(moved, shift, 1) if shift else moved
            row = moved if row is None else jnp.where(place == d, moved, row)
        rows.append(row)
    return rows


def fill_messages(tables, chosen, out_refs, lanes):
    column, place = lane_places(FACE_UP, lanes)
    for group, table in enumerate(tables):
        picked = pick(table, chosen(group))
        quads = []
        for quad in range(3):
            merged = picked[4 * quad * FACE_UP : (4 * quad + 1) * FACE_UP]
            for c in range(1, 4):
                f = 4 * quad + c
                if f < FIELDS:
                    merged = jnp.where(column == c, picked[f * FACE_UP : (f + 1) * FACE_UP], merged)
            quads.append(merged)
        messages = []
        for d in range(4):
            message = None
            for quad in range(3):
                shift = ((quad - d) * SLOT) % lanes
                moved = quads[quad] if shift == 0 else pltpu.roll(quads[quad], shift, 1)
                message = moved if message is None else jnp.where(place == quad, moved, message)
            messages.append(message)
        for axis, first in (("slab", 0), ("sub", 2)):
            even, _ = parity(axis)
            one, two = send_choice(even, messages[first], messages[first + 1])
            out_refs[first][group * FACE_UP : (group + 1) * FACE_UP, :] = one
            out_refs[first + 1][group * FACE_UP : (group + 1) * FACE_UP, :] = two


def face_operand(values):
    high, low = halves(values)
    return jnp.concatenate([high, high, low, jnp.zeros((SLOT, values.shape[1]), F32)], axis=0).astype(BF16)


def take_messages(in_refs, groups, far_ref, turn_ref, lanes):
    column, place = lane_places(FACE_UP, lanes)
    quads = []
    for group in range(groups):
        arrived = [ref[group * FACE_UP : (group + 1) * FACE_UP, :] for ref in in_refs]
        for axis, first in (("slab", 0), ("sub", 2)):
            _, even = parity(axis)
            arrived[first], arrived[first + 1] = send_choice(even, arrived[first + 1], arrived[first])
        for quad in range(3):
            merged = None
            for d in range(4):
                shift = ((d - quad) * SLOT) % lanes
                moved = arrived[d] if shift == 0 else pltpu.roll(arrived[d], shift, 1)
                merged = moved if merged is None else jnp.where(place == d, moved, merged)
            quads.append(merged)
    turned = jnp.dot(turn_ref[...], face_operand(jnp.concatenate(quads, axis=1)), preferred_element_type=F32)
    high, low = halves(turned)
    lefts = []
    for part in (high, low):
        columns = []
        for group in range(groups):
            for which in range(3):
                rows = slice(which * FACE_UP, (which + 1) * FACE_UP)
                pieces = []
                for f in range(FIELDS):
                    at = (3 * group + f // 4) * lanes
                    pieces.append(jnp.where(column == f % 4, part[rows, at : at + lanes], 0.0))
                pieces.append(jnp.zeros((FACE_UP, lanes), F32))
                columns.append(jnp.concatenate(pieces, axis=0))
        lefts.append(jnp.concatenate(columns, axis=1))
    left = jnp.concatenate(lefts, axis=0).astype(BF16)
    out = jnp.dot(left, far_ref[0 : 3 * groups * lanes, :], preferred_element_type=F32)
    return out[:ROWS] + out[ROWS:]


def gather_faces(in_refs, groups, near_ref, far_ref, turn_ref, aplus_ref, c_ref, lanes):
    half = lanes // 2
    low = low_half((FACE_UP, lanes), half)
    values = near_ref[...] + take_messages(in_refs, groups, far_ref, turn_ref, lanes)
    for group in GROUPS:
        fields = [g for q in group for g in (2 * q, 2 * q + 1) if g < FIELDS]
        for k in range(2):
            sums = {}
            for f in range(FIELDS):
                part = values[f * FACE_UP : (f + 1) * FACE_UP, k * lanes : (k + 1) * lanes]
                for g in fields:
                    term = aplus_ref[f * FIELDS + g, k : k + 1, :] * part
                    sums[g] = sums[g] + term if g in sums else term
            for q in group:
                first = sums[2 * q]
                second = sums[min(2 * q + 1, FIELDS - 1)]
                crossed = swap(jnp.where(low, second, first), half)
                sides = jnp.concatenate([jnp.where(low, first, crossed), jnp.where(low, crossed, second)], axis=0)
                high = sides.astype(BF16)
                rest = (sides - high.astype(F32)).astype(BF16)
                at, cols = 2 * k * FACE_UP, slice(q * lanes, (q + 1) * lanes)
                c_ref[at : at + 2 * FACE_UP, cols] = high
                c_ref[4 * FACE_UP + at : 4 * FACE_UP + at + 2 * FACE_UP, cols] = high
                c_ref[8 * FACE_UP + at : 8 * FACE_UP + at + 2 * FACE_UP, cols] = rest


def updated(c_ref, lift_ref, base_ref, finished, group, lanes):
    cols = span(group, lanes)
    outer = jnp.dot(lift_ref[...], c_ref[:, cols], preferred_element_type=F32)
    before = base_ref[:, cols]
    done = finished if len(group) == 1 else jnp.concatenate([finished, finished], axis=1)
    return jnp.where(done, before - outer, before)


def pack_coefs(ref, dirs, base, out_ref):
    for q in range(PAIRS - 1):
        for g in range(FIELDS):
            out_ref[q * FIELDS + g, base : base + dirs, :] = pair(ref[2 * q, g], ref[2 * q + 1, g])


def pack_last(lines, g, out_ref):
    for i in range(0, len(lines), 2):
        other = lines[i + 1] if i + 1 < len(lines) else jnp.zeros_like(lines[i])
        out_ref[(PAIRS - 1) * FIELDS + g, i // 2 : i // 2 + 1, :] = pair(lines[i], other)


def first_kernel(
    state_hbm, star_hbm, ck_hbm, project_hbm, cluster_hbm, elem_hbm, face_hbm,
    aminus_hbm, aplus_hbm, vol_hbm, flux_hbm, lift_hbm, rotate_hbm, neighbour_hbm, orient_hbm,
    m0, m1, m2, m3, packed_ref, star_out, ck_out, proj_out, i_ref, table_ref, send_out, star_ref, cluster_ref,
    aminus_out, aplus_out, vol_out, flux_out, lift_out, rotate_out, neighbour_out, orient_out,
    state_ref, ck_ref, project_ref, elem_ref, face_ref, weight_ref, faces_ref, m_ref, early, late, *, lanes,
):
    soon = [
        pltpu.make_async_copy(source, target, early.at[i])
        for i, (source, target) in enumerate((
            (cluster_hbm, cluster_ref), (ck_hbm, ck_ref), (state_hbm, state_ref), (star_hbm, star_ref),
            (project_hbm, project_ref), (elem_hbm, elem_ref), (face_hbm, face_ref),
        ))
    ]
    then = [
        pltpu.make_async_copy(source, target, late.at[i])
        for i, (source, target) in enumerate((
            (aminus_hbm, aminus_out), (aplus_hbm, aplus_out), (vol_hbm, vol_out), (flux_hbm, flux_out),
            (lift_hbm, lift_out), (rotate_hbm, rotate_out), (neighbour_hbm, neighbour_out), (orient_hbm, orient_out),
        ))
    ]
    for copy in soon + then:
        copy.start()
    for copy in soon:
        copy.wait()
    for q in range(PAIRS):
        packed_ref[:, q * lanes : (q + 1) * lanes] = pair(state_ref[2 * q], state_ref[min(2 * q + 1, FIELDS - 1)])
    pack_coefs(star_ref, 3, 0, star_out)
    for g in range(FIELDS):
        both = star_ref[FIELDS - 1, g]
        pack_last([both[d : d + 1] for d in range(3)], g, star_out)
    ck_out[...] = left_parts(-ck_ref[...].reshape(3 * MODES, MODES), MODES_UP).astype(BF16)
    proj_rows = [pad_rows(project_ref[:, j, :], FACE_UP) for j in range(4)]
    proj_out[...] = left_parts(jnp.concatenate(proj_rows, axis=0), MODES_UP).astype(BF16)
    rows = send_rows(face_ref, elem_ref, lanes)
    for i, row in enumerate(rows):
        send_out[i : i + 1, :] = row
    store_weights(weight_ref, pair(cluster_ref[...], cluster_ref[...]), 0)

    def state_of(group):
        return packed_ref[:, span(group, lanes)]

    predict(state_of, ck_out, star_out, weight_ref, proj_out, faces_ref, m_ref, i_ref, lanes)
    fill_table(faces_ref, table_ref, lanes)
    fill_messages([table_ref[...]], lambda group: one_hot(rows[0], 2 * lanes), (m0, m1, m2, m3), lanes)
    for copy in then:
        copy.wait()


def prepare_kernel(
    star_ref, aminus_ref, aplus_ref, vol_ref, flux_ref, lift_ref, rotate_ref, neighbour_ref, orient_ref, send_ref,
    coef_out, aplus_out, left_out, lift_out, turn_out, near_out, far_out, send_out, *, lanes,
):
    half = lanes // 2
    pack_coefs(star_ref, 3, 0, coef_out)
    pack_coefs(aminus_ref, 4, 3, coef_out)
    for g in range(FIELDS):
        ahead, behind = star_ref[FIELDS - 1, g], aminus_ref[FIELDS - 1, g]
        pack_last([ahead[d : d + 1] for d in range(3)] + [behind[j : j + 1] for j in range(4)], g, coef_out)
        for f in range(FIELDS):
            own = aplus_ref[f, g]
            for k in range(2):
                aplus_out[f * FIELDS + g, k : k + 1, :] = pair(own[2 * k : 2 * k + 1], own[2 * k + 1 : 2 * k + 2])
    both = jnp.concatenate([vol_ref[...].reshape(3 * MODES, MODES), -flux_ref[...].reshape(4 * MODES, MODES)], axis=0)
    left_out[...] = left_parts(both, MODES_UP).astype(BF16)
    lift = jnp.concatenate([pad_rows(lift_ref[:, j, :], FACE_UP) for j in range(4)], axis=0)
    lift = jnp.concatenate([lift, jnp.zeros((4 * FACE_UP, lanes - MODES), F32)], axis=1)
    lift = jnp.transpose(pad_rows(lift, lanes))[0:MODES, 0 : 4 * FACE_UP]
    lift_out[...] = left_parts(lift, 4 * FACE_UP).astype(BF16)
    turns = jnp.concatenate([pad_rows(rotate_ref[which], FACE_UP) for which in range(3)], axis=0)
    turn_out[...] = jnp.concatenate([left_parts(turns, FACE_UP), jnp.zeros((3 * FACE_UP, SLOT), F32)], axis=1).astype(BF16)
    row = jnp.concatenate([neighbour_ref[j : j + 1, :] for j in range(4)], axis=1)
    turned = jnp.concatenate([orient_ref[j : j + 1, :] for j in range(4)], axis=1)
    near_out[...] = one_hot(row, 4 * half)
    sub = lax.broadcasted_iota(jnp.int32, (lanes, 4 * half), 0)
    for group in range(4):
        target = 4 * half + ((sub // SLOT) % 4) * (4 * SLOT) + group * SLOT + sub % SLOT
        for which in range(3):
            at = (3 * group + which) * lanes
            hit = (target == row) & (turned == which)
            far_out[at : at + lanes, :] = jnp.where(hit, 1.0, 0.0).astype(BF16)
    for group in range(send_ref.shape[0]):
        send_out[:, group * lanes : (group + 1) * lanes] = one_hot(send_ref[group : group + 1, :], 4 * half)


def local_kernel(
    i_ref, packed_ref, table_ref, cluster_ref, coef_ref, left_ref, near_ref, turn_ref, orient_ref, own_ref, seen_ref,
    base_out, own_out, seen_out, m_ref, *, lanes, tick,
):
    cluster = pair(cluster_ref[...], cluster_ref[...])
    offset, finished = timing(cluster, tick)
    two = jnp.concatenate([offset, offset], axis=1)
    for group in GROUPS:
        cols = span(group, lanes)
        values = i_ref[:, cols]
        if tick:
            fresh = (offset if len(group) == 1 else two) == 0
            values = jnp.where(fresh, values, own_ref[:, cols] + values)
        own_out[:, cols] = values
        products(m_ref, 0, left_ref[...], values, 7, group, lanes)
    seen = pick(table_ref[...], near_ref[...])
    which = jnp.concatenate([orient_ref[j : j + 1, :] for j in range(4)], axis=1)
    for f in range(FIELDS):
        rows = slice(f * FACE_UP, (f + 1) * FACE_UP)
        turned = jnp.dot(turn_ref[...], face_operand(seen[rows]), preferred_element_type=F32)
        part = jnp.where(
            which == 0,
            turned[0:FACE_UP],
            jnp.where(which == 1, turned[FACE_UP : 2 * FACE_UP], turned[2 * FACE_UP : 3 * FACE_UP]),
        )
        seen_out[rows, :] = jnp.where(two == 0, part, seen_ref[rows, :] + part) if tick else part
    seen_out[FIELDS * FACE_UP :, :] = jnp.zeros((ROWS - FIELDS * FACE_UP, 2 * lanes), F32)
    for group in GROUPS:
        cols = span(group, lanes)
        before = packed_ref[:, cols]
        change = contract(m_ref, 0, coef_ref, 7, group, lanes)
        done = finished if len(group) == 1 else jnp.concatenate([finished, finished], axis=1)
        base_out[:, cols] = jnp.where(done, before + change, before)


def tick_kernel(
    r0, r1, r2, r3, near_ref, far_ref, turn_ref, aplus_ref, lift_ref, base_ref, cluster_ref,
    ck_ref, proj_ref, star_ref, send_ref, *rest, lanes, tick, olds, groups,
):
    old_refs = rest[:olds]
    m0, m1, m2, m3, packed_ref, i_ref, table_ref = rest[olds : olds + 7]
    rest = rest[olds + 7 :]
    sum_ref = None
    if tick == 1:
        sum_ref, rest = rest[0], rest[1:]
    weight_ref, faces_ref, m_ref, c_ref = rest
    cluster = pair(cluster_ref[...], cluster_ref[...])
    _, finished = timing(cluster, tick - 1)
    store_weights(weight_ref, cluster, tick)
    gather_faces((r0, r1, r2, r3), groups, near_ref, far_ref, turn_ref, aplus_ref, c_ref, lanes)

    def state_of(group):
        values = updated(c_ref, lift_ref, base_ref, finished, group, lanes)
        packed_ref[:, span(group, lanes)] = values
        return values

    predict(state_of, ck_ref, star_ref, weight_ref, proj_ref, faces_ref, m_ref, i_ref, lanes)
    fill_table(faces_ref, table_ref, lanes)
    table = table_ref[...]
    tables = [table]
    if tick == 1:
        two = old_refs[0][...] + table
        sum_ref[...] = two
        tables.append(two)
    if tick == 3:
        two = old_refs[0][...] + table
        four = old_refs[1][...] + two
        tables += [two, four, four]
    fill_messages(tables, lambda group: send_ref[:, group * lanes : (group + 1) * lanes], (m0, m1, m2, m3), lanes)


def last_kernel(
    r0, r1, r2, r3, near_ref, far_ref, turn_ref, aplus_ref, lift_ref, base_ref, cluster_ref, out_ref, c_ref, *, lanes,
):
    half = lanes // 2
    _, finished = timing(pair(cluster_ref[...], cluster_ref[...]), TICKS - 1)
    gather_faces((r0, r1, r2, r3), 4, near_ref, far_ref, turn_ref, aplus_ref, c_ref, lanes)
    for group in GROUPS:
        values = updated(c_ref, lift_ref, base_ref, finished, group, lanes)
        for i, q in enumerate(group):
            for side in range(2):
                if 2 * q + side < FIELDS:
                    out_ref[2 * q + side] = values[:, i * lanes + side * half : i * lanes + (side + 1) * half]


def call(body, outs, scratch, name, flops, arrays, far=False):
    moved = sum(a.size * a.dtype.itemsize for a in arrays)
    space = pltpu.MemorySpace.HBM if far else pltpu.VMEM
    if far:
        arrays = [pltpu.with_memory_space_constraint(x, pltpu.MemorySpace.HBM) for x in arrays]
    return pl.pallas_call(
        body,
        out_shape=outs,
        in_specs=[pl.BlockSpec(memory_space=space)] * len(arrays),
        out_specs=[pl.BlockSpec(memory_space=pltpu.VMEM)] * len(outs),
        scratch_shapes=scratch,
        compiler_params=pltpu.CompilerParams(vmem_limit_bytes=24 << 20),
        cost_estimate=pl.CostEstimate(flops=flops, bytes_accessed=moved, transcendentals=0),
        name=name,
    )(*arrays)


def shards(
    state, star, aminus, aplus, ck_stiff, vol_stiff, flux_local, lift, rotate, project,
    cluster, orient, neighbour, send_elem, send_face,
):
    elems = state.shape[-1]
    lanes = 2 * elems
    wide = PAIRS * lanes
    groups = send_elem.shape[1] // SLOT
    shape = jax.ShapeDtypeStruct
    cluster_row = cluster.reshape(1, elems)
    star, aminus, aplus = (jnp.transpose(x, (1, 2, 0, 3)) for x in (star, aminus, aplus))
    project = jnp.transpose(project, (1, 0, 2))
    lift = jnp.transpose(lift, (2, 0, 1))

    modal = shape((MODES, wide), F32)
    table = shape((ROWS, 4 * elems), F32)
    weights = pltpu.VMEM((SLOT, lanes), F32)
    faces = pltpu.VMEM((4 * FACE_UP, wide), F32)
    staged = pltpu.VMEM((2, 3 * MODES, wide), F32)
    sides = pltpu.VMEM((12 * FACE_UP, wide), BF16)

    def like(x):
        return shape(x.shape, x.dtype)

    def room(x):
        return pltpu.VMEM(x.shape, x.dtype)

    def message(count):
        return [shape((count * FACE_UP, lanes), F32)] * 4

    late = (aminus, aplus, vol_stiff, flux_local, lift, rotate, neighbour, orient)
    out = call(
        functools.partial(first_kernel, lanes=lanes),
        message(1)
        + [
            modal,
            shape((PAIRS * FIELDS, 3, lanes), F32),
            shape((3 * MODES, 3 * MODES_UP), BF16),
            shape((4 * FACE_UP, 3 * MODES_UP), BF16),
            modal,
            table,
            shape((groups, lanes), jnp.int32),
            like(star),
            like(cluster_row),
        ]
        + [like(x) for x in late],
        [room(state), room(ck_stiff), room(project), room(send_elem), room(send_face), weights, faces, staged]
        + [pltpu.SemaphoreType.DMA((7,)), pltpu.SemaphoreType.DMA((len(late),))],
        "first", 400_000_000,
        (state, star, ck_stiff, project, cluster_row, send_elem, send_face, *late), far=True,
    )
    messages, out = out[:4], out[4:]
    packed, star_pairs, ck_left, proj_left, integral, table_now, send, star, cluster_row = out[:9]
    late = out[9:]
    orient = late[-1]
    coef, aplus_pairs, left, lift_left, turn, near_hot, far_hot, send_hot = call(
        functools.partial(prepare_kernel, lanes=lanes),
        [
            shape((PAIRS * FIELDS, 7, lanes), F32),
            shape((FIELDS * FIELDS, 2, lanes), F32),
            shape((7 * MODES, 3 * MODES_UP), BF16),
            shape((MODES, 12 * FACE_UP), BF16),
            shape((3 * FACE_UP, 80), BF16),
            shape((4 * elems, 4 * elems), BF16),
            shape((12 * lanes, 4 * elems), BF16),
            shape((4 * elems, groups * lanes), BF16),
        ],
        [],
        "prepare", 100_000_000,
        (star, *late, send),
    )
    own = integral
    seen = table_now
    two = None
    for tick in range(TICKS):
        arrived = [None] * 4
        for slot, axis, phase in ((1, "slab", 1), (0, "slab", 0), (3, "sub", 1), (2, "sub", 0)):
            arrived[slot] = exchange(messages[slot], axis, phase)
        base, own, seen = call(
            functools.partial(local_kernel, lanes=lanes, tick=tick),
            [modal, modal, table],
            [pltpu.VMEM((1, 7 * MODES, wide), F32)],
            f"local{tick}", 300_000_000,
            (integral, packed, table_now, cluster_row, coef, left, near_hot, turn, orient, own, seen),
        )
        count = (1, 2, 1, 4)[tick]
        common = (*arrived, seen, far_hot, turn, aplus_pairs, lift_left, base, cluster_row)
        if tick == TICKS - 1:
            return call(
                functools.partial(last_kernel, lanes=lanes),
                [shape(state.shape, F32)],
                [sides],
                "last", 100_000_000, common,
            )[0]
        olds = {0: (table_now,), 1: (), 2: (table_now, two)}[tick]
        sends = (1, 2, 1, 4)[tick + 1]
        out = call(
            functools.partial(tick_kernel, lanes=lanes, tick=tick + 1, olds=len(olds), groups=count),
            message(sends) + [modal, modal, table] + ([table] if tick == 0 else []),
            [weights, faces, staged, sides],
            f"tick{tick + 1}", 500_000_000,
            (*common, ck_left, proj_left, star_pairs, send_hot, *olds),
        )
        messages, (packed, integral, table_now) = out[:4], out[4:7]
        if tick == 0:
            two = out[7]


def solution(mesh):
    placed = (
        P(None, None, ("slab", "sub")),
        P(None, None, None, ("slab", "sub")),
        P(None, None, None, ("slab", "sub")),
        P(None, None, None, ("slab", "sub")),
        P(),
        P(),
        P(),
        P(),
        P(),
        P(),
        P(("slab", "sub")),
        P(None, ("slab", "sub")),
        P(None, ("slab", "sub")),
        P(None, ("slab", "sub")),
        P(None, ("slab", "sub")),
    )
    return jax.shard_map(
        shards,
        mesh=mesh,
        in_specs=placed,
        out_specs=P(None, None, ("slab", "sub")),
        check_vma=False,
    )
```

```python
import functools

import jax
import jax.numpy as jnp
from jax import lax
from jax.experimental import pallas as pl
from jax.experimental.pallas import tpu as pltpu
from jax.sharding import PartitionSpec as P

FIELDS = 9
PAIRS = 5
MODES = 56
MODES_UP = 64
FACE_MODES = 21
FACE_UP = 24
ROWS = 2 * PAIRS * FACE_UP
DERIVS = 6
TICKS = 4
SLOT = 8
TIME_STEP = 1.0
F32 = jnp.float32
BF16 = jnp.bfloat16
BLOCKS = ((0, 32), (32, 24))
GROUPS = ((0, 1), (2, 3), (4,))


def paired(axis):
    return lax.axis_size(axis) % 2 == 0


def exchange(x, axis, phase):
    size = lax.axis_size(axis)
    if paired(axis):
        pairs = []
        for i in range(phase, size + phase, 2):
            one, two = i % size, (i + 1) % size
            pairs += [(one, two), (two, one)]
    else:
        by = 1 if phase == 0 else -1
        pairs = [(i, (i + by) % size) for i in range(size)]
    return lax.ppermute(x, axis, pairs)


def taylor_constants():
    width = TIME_STEP / TICKS
    table = []
    for begin in range(TICKS):
        factorial = 1.0
        row = []
        for order in range(DERIVS):
            factorial = factorial * (order + 1)
            span = float((begin + 1) ** (order + 1) - begin ** (order + 1))
            row.append(span * width ** (order + 1) / factorial)
        table.append(row)
    return table


def low_half(shape, half):
    return lax.broadcasted_iota(jnp.int32, shape, len(shape) - 1) < half


def swap(x, half):
    return pltpu.roll(x, half, x.ndim - 1)


def pair(a, b):
    return jnp.concatenate([a, b], axis=-1)


def halves(x):
    high = x.astype(BF16).astype(F32)
    return high, x - high


def pad_rows(x, rows):
    if x.shape[0] == rows:
        return x
    return jnp.concatenate([x, jnp.zeros((rows - x.shape[0], x.shape[1]), x.dtype)], axis=0)


def timing(cluster, tick):
    period = jnp.where(cluster == 0, 4, jnp.where(cluster == 1, 2, 1))
    offset = jnp.where(cluster == 0, tick % 4, jnp.where(cluster == 1, tick % 2, 0))
    return offset, offset == period - 1


def right_operand(values):
    values = pad_rows(values, MODES_UP)
    high = values.astype(BF16)
    low = (values - high.astype(F32)).astype(BF16)
    return jnp.concatenate([high, high, low], axis=0)


def left_parts(matrix, up):
    rows = matrix.shape[0]
    if up > matrix.shape[1]:
        matrix = jnp.concatenate([matrix, jnp.zeros((rows, up - matrix.shape[1]), F32)], axis=1)
    high, low = halves(matrix)
    return jnp.concatenate([high, low, high], axis=1)


def send_choice(even, forward, backward):
    return jnp.where(even, forward, backward), jnp.where(even, backward, forward)


def parity(axis):
    if not paired(axis):
        return True, False
    even = lax.rem(lax.axis_index(axis), 2) == 0
    return even, even


def products(m_ref, slot, left, values, dirs, group, lanes):
    out = jnp.dot(left, right_operand(values), preferred_element_type=F32)
    if group == GROUPS[-1]:
        low = low_half((MODES, lanes), lanes // 2)
        for i in range(0, dirs, 2):
            one = out[i * MODES : (i + 1) * MODES]
            if i + 1 < dirs:
                one = jnp.where(low, one, out[(i + 1) * MODES : (i + 2) * MODES])
            m_ref[slot][-1][(i // 2) * MODES : (i // 2 + 1) * MODES, :] = one
    else:
        m_ref[slot][GROUPS.index(group)][...] = out


def contract(m_ref, slot, coef_ref, dirs, group, lanes):
    half = lanes // 2
    fields = [g for q in group for g in (2 * q, 2 * q + 1) if g < FIELDS]
    terms = [(d, q, q, d) for q in range(PAIRS - 1) for d in range(dirs)]
    terms += [(i, PAIRS - 1, PAIRS - 1, i) for i in range((dirs + 1) // 2)]
    columns = {q: [] for q in group}
    for row, count in BLOCKS:
        sums = {}
        for d, q, block, line in terms:
            at = (q % 2) * lanes
            values = m_ref[slot][q // 2][d * MODES + row : d * MODES + row + count, at : at + lanes]
            for g in fields:
                term = coef_ref[block * FIELDS + g, line : line + 1, :] * values
                sums[g] = sums[g] + term if g in sums else term
        low = low_half((count, lanes), half)
        for q in group:
            first = sums[2 * q]
            if 2 * q + 1 < FIELDS:
                second = sums[2 * q + 1]
                result = jnp.where(low, first, second) + swap(jnp.where(low, second, first), half)
            else:
                result = first + swap(first, half)
            columns[q].append(result)
    columns = [jnp.concatenate(columns[q], axis=0) for q in group]
    return columns[0] if len(columns) == 1 else jnp.concatenate(columns, axis=1)


def span(group, lanes):
    return slice(group[0] * lanes, (group[-1] + 1) * lanes)


def predict(state_of, ck_ref, star_ref, weight_ref, proj_ref, face_ref, m_ref, i_ref, lanes):
    def weight(order, group):
        row = weight_ref[order : order + 1, :]
        return row if len(group) == 1 else pair(row, row)

    for group in GROUPS:
        values = state_of(group)
        i_ref[:, span(group, lanes)] = weight(0, group) * values
        products(m_ref, 0, ck_ref[...], values, 3, group, lanes)
    for order in range(1, DERIVS):
        for group in GROUPS:
            values = contract(m_ref, (order - 1) % 2, star_ref, 3, group, lanes)
            total = i_ref[:, span(group, lanes)] + weight(order, group) * values
            i_ref[:, span(group, lanes)] = total
            if order < DERIVS - 1:
                products(m_ref, order % 2, ck_ref[...], values, 3, group, lanes)
            else:
                face_ref[:, span(group, lanes)] = jnp.dot(
                    proj_ref[...], right_operand(total), preferred_element_type=F32
                )


def store_weights(weight_ref, cluster, tick):
    offset, _ = timing(cluster, tick)
    table = taylor_constants()
    for order in range(DERIVS):
        row = jnp.full(cluster.shape, table[0][order], F32)
        for begin in range(1, TICKS):
            row = jnp.where(offset == begin, table[begin][order], row)
        weight_ref[order : order + 1, :] = row


def fill_table(face_ref, table_ref, lanes):
    half = lanes // 2
    low = low_half((FACE_UP, lanes), half)
    for q in range(PAIRS):
        for k in range(2):
            one = face_ref[2 * k * FACE_UP : (2 * k + 1) * FACE_UP, q * lanes : (q + 1) * lanes]
            two = face_ref[(2 * k + 1) * FACE_UP : (2 * k + 2) * FACE_UP, q * lanes : (q + 1) * lanes]
            crossed = swap(jnp.where(low, two, one), half)
            table_ref[2 * q * FACE_UP : (2 * q + 1) * FACE_UP, k * lanes : (k + 1) * lanes] = jnp.where(low, one, crossed)
            table_ref[(2 * q + 1) * FACE_UP : (2 * q + 2) * FACE_UP, k * lanes : (k + 1) * lanes] = jnp.where(
                low, crossed, two
            )


def pick(table, chosen):
    rows = table.shape[0]
    high, low = halves(table)
    both = jnp.concatenate([high, low], axis=0).astype(BF16)
    out = jnp.dot(both, chosen, preferred_element_type=F32)
    return out[:rows] + out[rows:]


def one_hot(index_row, rows):
    sub = lax.broadcasted_iota(jnp.int32, (rows, index_row.shape[1]), 0)
    return jnp.where(sub == index_row, 1.0, 0.0).astype(BF16)


def lane_places(rows, lanes):
    lane = lax.broadcasted_iota(jnp.int32, (rows, lanes), 1)
    return lane // (4 * SLOT), (lane // SLOT) % 4


def send_rows(face_ref, elem_ref, lanes):
    slots = face_ref.shape[1]
    half = lanes // 2
    index = face_ref[...] * half + elem_ref[...]
    index = jnp.concatenate([index] * (lanes // slots), axis=1)
    _, place = lane_places(1, lanes)
    rows = []
    for group in range(slots // SLOT):
        row = None
        for d in range(4):
            shift = ((d - group) * SLOT) % lanes
            moved = index[d : d + 1, :]
            moved = pltpu.roll(moved, shift, 1) if shift else moved
            row = moved if row is None else jnp.where(place == d, moved, row)
        rows.append(row)
    return rows


def fill_messages(tables, chosen, out_refs, lanes):
    column, place = lane_places(FACE_UP, lanes)
    for group, table in enumerate(tables):
        picked = pick(table, chosen(group))
        quads = []
        for quad in range(3):
            merged = picked[4 * quad * FACE_UP : (4 * quad + 1) * FACE_UP]
            for c in range(1, 4):
                f = 4 * quad + c
                if f < FIELDS:
                    merged = jnp.where(column == c, picked[f * FACE_UP : (f + 1) * FACE_UP], merged)
            quads.append(merged)
        messages = []
        for d in range(4):
            message = None
            for quad in range(3):
                shift = ((quad - d) * SLOT) % lanes
                moved = quads[quad] if shift == 0 else pltpu.roll(quads[quad], shift, 1)
                message = moved if message is None else jnp.where(place == quad, moved, message)
            messages.append(message)
        for axis, first in (("slab", 0), ("sub", 2)):
            even, _ = parity(axis)
            one, two = send_choice(even, messages[first], messages[first + 1])
            out_refs[first][group * FACE_UP : (group + 1) * FACE_UP, :] = one
            out_refs[first + 1][group * FACE_UP : (group + 1) * FACE_UP, :] = two


def face_operand(values):
    high, low = halves(values)
    return jnp.concatenate([high, high, low, jnp.zeros((SLOT, values.shape[1]), F32)], axis=0).astype(BF16)


def take_messages(in_refs, groups, far_ref, turn_ref, lanes):
    column, place = lane_places(FACE_UP, lanes)
    quads = []
    for group in range(groups):
        arrived = [ref[group * FACE_UP : (group + 1) * FACE_UP, :] for ref in in_refs]
        for axis, first in (("slab", 0), ("sub", 2)):
            _, even = parity(axis)
            arrived[first], arrived[first + 1] = send_choice(even, arrived[first + 1], arrived[first])
        for quad in range(3):
            merged = None
            for d in range(4):
                shift = ((d - quad) * SLOT) % lanes
                moved = arrived[d] if shift == 0 else pltpu.roll(arrived[d], shift, 1)
                merged = moved if merged is None else jnp.where(place == d, moved, merged)
            quads.append(merged)
    turned = jnp.dot(turn_ref[...], face_operand(jnp.concatenate(quads, axis=1)), preferred_element_type=F32)
    high, low = halves(turned)
    lefts = []
    for part in (high, low):
        columns = []
        for group in range(groups):
            for which in range(3):
                rows = slice(which * FACE_UP, (which + 1) * FACE_UP)
                pieces = []
                for f in range(FIELDS):
                    at = (3 * group + f // 4) * lanes
                    pieces.append(jnp.where(column == f % 4, part[rows, at : at + lanes], 0.0))
                pieces.append(jnp.zeros((FACE_UP, lanes), F32))
                columns.append(jnp.concatenate(pieces, axis=0))
        lefts.append(jnp.concatenate(columns, axis=1))
    left = jnp.concatenate(lefts, axis=0).astype(BF16)
    out = jnp.dot(left, far_ref[0 : 3 * groups * lanes, :], preferred_element_type=F32)
    return out[:ROWS] + out[ROWS:]


def gather_faces(in_refs, groups, near_ref, far_ref, turn_ref, aplus_ref, c_ref, lanes):
    half = lanes // 2
    low = low_half((FACE_UP, lanes), half)
    values = near_ref[...] + take_messages(in_refs, groups, far_ref, turn_ref, lanes)
    for group in GROUPS:
        fields = [g for q in group for g in (2 * q, 2 * q + 1) if g < FIELDS]
        for k in range(2):
            sums = {}
            for f in range(FIELDS):
                part = values[f * FACE_UP : (f + 1) * FACE_UP, k * lanes : (k + 1) * lanes]
                for g in fields:
                    term = aplus_ref[f * FIELDS + g, k : k + 1, :] * part
                    sums[g] = sums[g] + term if g in sums else term
            for q in group:
                first = sums[2 * q]
                second = sums[min(2 * q + 1, FIELDS - 1)]
                crossed = swap(jnp.where(low, second, first), half)
                sides = jnp.concatenate([jnp.where(low, first, crossed), jnp.where(low, crossed, second)], axis=0)
                high = sides.astype(BF16)
                rest = (sides - high.astype(F32)).astype(BF16)
                at, cols = 2 * k * FACE_UP, slice(q * lanes, (q + 1) * lanes)
                c_ref[at : at + 2 * FACE_UP, cols] = high
                c_ref[4 * FACE_UP + at : 4 * FACE_UP + at + 2 * FACE_UP, cols] = high
                c_ref[8 * FACE_UP + at : 8 * FACE_UP + at + 2 * FACE_UP, cols] = rest


def updated(c_ref, lift_ref, base_ref, finished, group, lanes):
    cols = span(group, lanes)
    outer = jnp.dot(lift_ref[...], c_ref[:, cols], preferred_element_type=F32)
    before = base_ref[:, cols]
    done = finished if len(group) == 1 else jnp.concatenate([finished, finished], axis=1)
    return jnp.where(done, before - outer, before)


def pack_coefs(ref, dirs, base, out_ref):
    for q in range(PAIRS - 1):
        for g in range(FIELDS):
            out_ref[q * FIELDS + g, base : base + dirs, :] = pair(ref[2 * q, g], ref[2 * q + 1, g])


def pack_last(lines, g, out_ref):
    for i in range(0, len(lines), 2):
        other = lines[i + 1] if i + 1 < len(lines) else jnp.zeros_like(lines[i])
        out_ref[(PAIRS - 1) * FIELDS + g, i // 2 : i // 2 + 1, :] = pair(lines[i], other)


def first_kernel(
    state_hbm, star_hbm, ck_hbm, project_hbm, cluster_hbm, elem_hbm, face_hbm,
    aminus_hbm, aplus_hbm, vol_hbm, flux_hbm, lift_hbm, rotate_hbm, neighbour_hbm, orient_hbm,
    packed_ref, star_out, ck_out, proj_out, send_out, star_ref, cluster_ref,
    aminus_out, aplus_out, vol_out, flux_out, lift_out, rotate_out, neighbour_out, orient_out,
    state_ref, ck_ref, project_ref, elem_ref, face_ref, early, late, *, lanes,
):
    soon = [
        pltpu.make_async_copy(source, target, early.at[i])
        for i, (source, target) in enumerate((
            (state_hbm, state_ref), (star_hbm, star_ref), (ck_hbm, ck_ref), (cluster_hbm, cluster_ref),
            (project_hbm, project_ref), (elem_hbm, elem_ref), (face_hbm, face_ref),
        ))
    ]
    then = [
        pltpu.make_async_copy(source, target, late.at[i])
        for i, (source, target) in enumerate((
            (aminus_hbm, aminus_out), (aplus_hbm, aplus_out), (vol_hbm, vol_out), (flux_hbm, flux_out),
            (lift_hbm, lift_out), (rotate_hbm, rotate_out), (neighbour_hbm, neighbour_out), (orient_hbm, orient_out),
        ))
    ]
    for copy in soon + then:
        copy.start()
    for copy in soon:
        copy.wait()
    for q in range(PAIRS):
        packed_ref[:, q * lanes : (q + 1) * lanes] = pair(state_ref[2 * q], state_ref[min(2 * q + 1, FIELDS - 1)])
    pack_coefs(star_ref, 3, 0, star_out)
    for g in range(FIELDS):
        both = star_ref[FIELDS - 1, g]
        pack_last([both[d : d + 1] for d in range(3)], g, star_out)
    ck_out[...] = left_parts(-ck_ref[...].reshape(3 * MODES, MODES), MODES_UP).astype(BF16)
    proj_rows = [pad_rows(project_ref[:, j, :], FACE_UP) for j in range(4)]
    proj_out[...] = left_parts(jnp.concatenate(proj_rows, axis=0), MODES_UP).astype(BF16)
    for i, row in enumerate(send_rows(face_ref, elem_ref, lanes)):
        send_out[i : i + 1, :] = row
    for copy in then:
        copy.wait()


def predict_kernel(
    packed_ref, cluster_ref, ck_ref, star_ref, proj_ref, i_ref, faces_ref, weight_ref, m_ref, *, lanes, tick
):
    store_weights(weight_ref, pair(cluster_ref[...], cluster_ref[...]), tick)

    def state_of(group):
        return packed_ref[:, span(group, lanes)]

    predict(state_of, ck_ref, star_ref, weight_ref, proj_ref, faces_ref, m_ref, i_ref, lanes)


def send_kernel(faces_ref, send_ref, *rest, lanes, tick, olds):
    old_refs = rest[:olds]
    m0, m1, m2, m3, table_ref = rest[olds : olds + 5]
    fill_table(faces_ref, table_ref, lanes)
    table = table_ref[...]
    tables = [table]
    if tick == 1:
        two = old_refs[0][...] + table
        rest[olds + 5][...] = two
        tables.append(two)
    if tick == 3:
        two = old_refs[0][...] + table
        four = old_refs[1][...] + two
        tables += [two, four, four]

    def chosen(group):
        if tick:
            return send_ref[:, group * lanes : (group + 1) * lanes]
        return one_hot(send_ref[group : group + 1, :], 2 * lanes)

    fill_messages(tables, chosen, (m0, m1, m2, m3), lanes)


def prepare_kernel(
    star_ref, aminus_ref, aplus_ref, vol_ref, flux_ref, lift_ref, rotate_ref, neighbour_ref, orient_ref, send_ref,
    coef_out, aplus_out, left_out, lift_out, turn_out, near_out, far_out, send_out, *, lanes,
):
    half = lanes // 2
    pack_coefs(star_ref, 3, 0, coef_out)
    pack_coefs(aminus_ref, 4, 3, coef_out)
    for g in range(FIELDS):
        ahead, behind = star_ref[FIELDS - 1, g], aminus_ref[FIELDS - 1, g]
        pack_last([ahead[d : d + 1] for d in range(3)] + [behind[j : j + 1] for j in range(4)], g, coef_out)
        for f in range(FIELDS):
            own = aplus_ref[f, g]
            for k in range(2):
                aplus_out[f * FIELDS + g, k : k + 1, :] = pair(own[2 * k : 2 * k + 1], own[2 * k + 1 : 2 * k + 2])
    both = jnp.concatenate([vol_ref[...].reshape(3 * MODES, MODES), -flux_ref[...].reshape(4 * MODES, MODES)], axis=0)
    left_out[...] = left_parts(both, MODES_UP).astype(BF16)
    lift = jnp.concatenate([pad_rows(lift_ref[:, j, :], FACE_UP) for j in range(4)], axis=0)
    lift = jnp.concatenate([lift, jnp.zeros((4 * FACE_UP, lanes - MODES), F32)], axis=1)
    lift = jnp.transpose(pad_rows(lift, lanes))[0:MODES, 0 : 4 * FACE_UP]
    lift_out[...] = left_parts(lift, 4 * FACE_UP).astype(BF16)
    turns = jnp.concatenate([pad_rows(rotate_ref[which], FACE_UP) for which in range(3)], axis=0)
    turn_out[...] = jnp.concatenate([left_parts(turns, FACE_UP), jnp.zeros((3 * FACE_UP, SLOT), F32)], axis=1).astype(BF16)
    row = jnp.concatenate([neighbour_ref[j : j + 1, :] for j in range(4)], axis=1)
    turned = jnp.concatenate([orient_ref[j : j + 1, :] for j in range(4)], axis=1)
    near_out[...] = one_hot(row, 4 * half)
    sub = lax.broadcasted_iota(jnp.int32, (lanes, 4 * half), 0)
    for group in range(4):
        target = 4 * half + ((sub // SLOT) % 4) * (4 * SLOT) + group * SLOT + sub % SLOT
        for which in range(3):
            at = (3 * group + which) * lanes
            hit = (target == row) & (turned == which)
            far_out[at : at + lanes, :] = jnp.where(hit, 1.0, 0.0).astype(BF16)
    for group in range(send_ref.shape[0]):
        send_out[:, group * lanes : (group + 1) * lanes] = one_hot(send_ref[group : group + 1, :], 4 * half)


def local_kernel(
    i_ref, packed_ref, table_ref, cluster_ref, coef_ref, left_ref, near_ref, turn_ref, orient_ref, own_ref, seen_ref,
    base_out, own_out, seen_out, m_ref, *, lanes, tick,
):
    cluster = pair(cluster_ref[...], cluster_ref[...])
    offset, finished = timing(cluster, tick)
    two = jnp.concatenate([offset, offset], axis=1)
    for group in GROUPS:
        cols = span(group, lanes)
        values = i_ref[:, cols]
        if tick:
            fresh = (offset if len(group) == 1 else two) == 0
            values = jnp.where(fresh, values, own_ref[:, cols] + values)
        own_out[:, cols] = values
        products(m_ref, 0, left_ref[...], values, 7, group, lanes)
    seen = pick(table_ref[...], near_ref[...])
    which = jnp.concatenate([orient_ref[j : j + 1, :] for j in range(4)], axis=1)
    for f in range(FIELDS):
        rows = slice(f * FACE_UP, (f + 1) * FACE_UP)
        turned = jnp.dot(turn_ref[...], face_operand(seen[rows]), preferred_element_type=F32)
        part = jnp.where(
            which == 0,
            turned[0:FACE_UP],
            jnp.where(which == 1, turned[FACE_UP : 2 * FACE_UP], turned[2 * FACE_UP : 3 * FACE_UP]),
        )
        seen_out[rows, :] = jnp.where(two == 0, part, seen_ref[rows, :] + part) if tick else part
    seen_out[FIELDS * FACE_UP :, :] = jnp.zeros((ROWS - FIELDS * FACE_UP, 2 * lanes), F32)
    for group in GROUPS:
        cols = span(group, lanes)
        before = packed_ref[:, cols]
        change = contract(m_ref, 0, coef_ref, 7, group, lanes)
        done = finished if len(group) == 1 else jnp.concatenate([finished, finished], axis=1)
        base_out[:, cols] = jnp.where(done, before + change, before)


def update_kernel(
    r0, r1, r2, r3, near_ref, far_ref, turn_ref, aplus_ref, lift_ref, base_ref, cluster_ref, packed_ref, c_ref,
    *, lanes, tick, groups,
):
    _, finished = timing(pair(cluster_ref[...], cluster_ref[...]), tick)
    gather_faces((r0, r1, r2, r3), groups, near_ref, far_ref, turn_ref, aplus_ref, c_ref, lanes)
    for group in GROUPS:
        packed_ref[:, span(group, lanes)] = updated(c_ref, lift_ref, base_ref, finished, group, lanes)


def last_kernel(
    r0, r1, r2, r3, near_ref, far_ref, turn_ref, aplus_ref, lift_ref, base_ref, cluster_ref, out_ref, c_ref, *, lanes,
):
    half = lanes // 2
    _, finished = timing(pair(cluster_ref[...], cluster_ref[...]), TICKS - 1)
    gather_faces((r0, r1, r2, r3), 4, near_ref, far_ref, turn_ref, aplus_ref, c_ref, lanes)
    for group in GROUPS:
        values = updated(c_ref, lift_ref, base_ref, finished, group, lanes)
        for i, q in enumerate(group):
            for side in range(2):
                if 2 * q + side < FIELDS:
                    out_ref[2 * q + side] = values[:, i * lanes + side * half : i * lanes + (side + 1) * half]


def stages(slots, dirs, lanes):
    wide = pltpu.VMEM((dirs * MODES, 2 * lanes), F32)
    last = pltpu.VMEM(((dirs + 1) // 2 * MODES, lanes), F32)
    return [[wide, wide, last] for _ in range(slots)]


def call(body, outs, scratch, name, flops, arrays, far=False):
    moved = sum(a.size * a.dtype.itemsize for a in arrays)
    space = pltpu.MemorySpace.HBM if far else pltpu.VMEM
    if far:
        arrays = [pltpu.with_memory_space_constraint(x, pltpu.MemorySpace.HBM) for x in arrays]
    return pl.pallas_call(
        body,
        out_shape=outs,
        in_specs=[pl.BlockSpec(memory_space=space)] * len(arrays),
        out_specs=[pl.BlockSpec(memory_space=pltpu.VMEM)] * len(outs),
        scratch_shapes=scratch,
        compiler_params=pltpu.CompilerParams(vmem_limit_bytes=24 << 20),
        cost_estimate=pl.CostEstimate(flops=flops, bytes_accessed=moved, transcendentals=0),
        name=name,
    )(*arrays)


def shards(
    state, star, aminus, aplus, ck_stiff, vol_stiff, flux_local, lift, rotate, project,
    cluster, orient, neighbour, send_elem, send_face,
):
    elems = state.shape[-1]
    lanes = 2 * elems
    wide = PAIRS * lanes
    groups = send_elem.shape[1] // SLOT
    shape = jax.ShapeDtypeStruct
    cluster_row = cluster.reshape(1, elems)
    star, aminus, aplus = (jnp.transpose(x, (1, 2, 0, 3)) for x in (star, aminus, aplus))
    project = jnp.transpose(project, (1, 0, 2))
    lift = jnp.transpose(lift, (2, 0, 1))

    modal = shape((MODES, wide), F32)
    table = shape((ROWS, 4 * elems), F32)
    weights = pltpu.VMEM((SLOT, lanes), F32)
    faces = shape((4 * FACE_UP, wide), F32)
    staged = stages(2, 3, lanes)
    sides = pltpu.VMEM((12 * FACE_UP, wide), BF16)

    def like(x):
        return shape(x.shape, x.dtype)

    def room(x):
        return pltpu.VMEM(x.shape, x.dtype)

    def message(count):
        return [shape((count * FACE_UP, lanes), F32)] * 4

    late = (aminus, aplus, vol_stiff, flux_local, lift, rotate, neighbour, orient)
    packed, star_pairs, ck_left, proj_left, send, star, cluster_row, *late = call(
        functools.partial(first_kernel, lanes=lanes),
        [
            modal,
            shape((PAIRS * FIELDS, 3, lanes), F32),
            shape((3 * MODES, 3 * MODES_UP), BF16),
            shape((4 * FACE_UP, 3 * MODES_UP), BF16),
            shape((groups, lanes), jnp.int32),
            like(star),
            like(cluster_row),
        ]
        + [like(x) for x in late],
        [room(state), room(ck_stiff), room(project), room(send_elem), room(send_face)]
        + [pltpu.SemaphoreType.DMA((7,)), pltpu.SemaphoreType.DMA((len(late),))],
        "first", 10_000_000,
        (state, star, ck_stiff, project, cluster_row, send_elem, send_face, *late), far=True,
    )
    orient = late[-1]

    def predicted(tick, packed, chosen, olds):
        integral, face_values = call(
            functools.partial(predict_kernel, lanes=lanes, tick=tick),
            [modal, faces],
            [weights, staged],
            f"predict{tick}", 400_000_000,
            (packed, cluster_row, ck_left, star_pairs, proj_left),
        )
        out = call(
            functools.partial(send_kernel, lanes=lanes, tick=tick, olds=len(olds)),
            message((1, 2, 1, 4)[tick]) + [table] + ([table] if tick == 1 else []),
            [],
            f"send{tick}", 50_000_000,
            (face_values, chosen, *olds),
        )
        return integral, out[:4], out[4:]

    integral, messages, (table_now,) = predicted(0, packed, send, ())
    coef, aplus_pairs, left, lift_left, turn, near_hot, far_hot, send_hot = call(
        functools.partial(prepare_kernel, lanes=lanes),
        [
            shape((PAIRS * FIELDS, 7, lanes), F32),
            shape((FIELDS * FIELDS, 2, lanes), F32),
            shape((7 * MODES, 3 * MODES_UP), BF16),
            shape((MODES, 12 * FACE_UP), BF16),
            shape((3 * FACE_UP, 80), BF16),
            shape((4 * elems, 4 * elems), BF16),
            shape((12 * lanes, 4 * elems), BF16),
            shape((4 * elems, groups * lanes), BF16),
        ],
        [],
        "prepare", 100_000_000,
        (star, *late, send),
    )
    own = integral
    seen = table_now
    two = None
    for tick in range(TICKS):
        arrived = [None] * 4
        for slot, axis, phase in ((1, "slab", 1), (0, "slab", 0), (3, "sub", 1), (2, "sub", 0)):
            arrived[slot] = exchange(messages[slot], axis, phase)
        base, own, seen = call(
            functools.partial(local_kernel, lanes=lanes, tick=tick),
            [modal, modal, table],
            [stages(1, 7, lanes)],
            f"local{tick}", 300_000_000,
            (integral, packed, table_now, cluster_row, coef, left, near_hot, turn, orient, own, seen),
        )
        count = (1, 2, 1, 4)[tick]
        common = (*arrived, seen, far_hot, turn, aplus_pairs, lift_left, base, cluster_row)
        if tick == TICKS - 1:
            return call(
                functools.partial(last_kernel, lanes=lanes),
                [shape(state.shape, F32)],
                [sides],
                "last", 100_000_000, common,
            )[0]
        packed = call(
            functools.partial(update_kernel, lanes=lanes, tick=tick, groups=count),
            [modal],
            [sides],
            f"update{tick}", 100_000_000, common,
        )[0]
        olds = {0: (table_now,), 1: (), 2: (table_now, two)}[tick]
        integral, messages, tables = predicted(tick + 1, packed, send_hot, olds)
        table_now = tables[0]
        if tick == 0:
            two = tables[1]


def solution(mesh):
    placed = (
        P(None, None, ("slab", "sub")),
        P(None, None, None, ("slab", "sub")),
        P(None, None, None, ("slab", "sub")),
        P(None, None, None, ("slab", "sub")),
        P(),
        P(),
        P(),
        P(),
        P(),
        P(),
        P(("slab", "sub")),
        P(None, ("slab", "sub")),
        P(None, ("slab", "sub")),
        P(None, ("slab", "sub")),
        P(None, ("slab", "sub")),
    )
    return jax.shard_map(
        shards,
        mesh=mesh,
        in_specs=placed,
        out_specs=P(None, None, ("slab", "sub")),
        check_vma=False,
    )
```

```python
import functools

import jax
import jax.numpy as jnp
from jax import lax
from jax.experimental import pallas as pl
from jax.experimental.pallas import tpu as pltpu
from jax.sharding import PartitionSpec as P

FIELDS = 9
PAIRS = 5
MODES = 56
MODES_UP = 64
FACE_MODES = 21
FACE_UP = 24
ROWS = 2 * PAIRS * FACE_UP
DERIVS = 6
TICKS = 4
SLOT = 8
TIME_STEP = 1.0
F32 = jnp.float32
BF16 = jnp.bfloat16
BLOCKS = ((0, 32), (32, 24))
GROUPS = ((0, 1), (2, 3), (4,))
GROUPS_AT = (1, 2, 1, 4)


def paired(axis):
    return lax.axis_size(axis) % 2 == 0


def exchange(x, axis, phase):
    size = lax.axis_size(axis)
    if paired(axis):
        pairs = []
        for i in range(phase, size + phase, 2):
            one, two = i % size, (i + 1) % size
            pairs += [(one, two), (two, one)]
    else:
        by = 1 if phase == 0 else -1
        pairs = [(i, (i + by) % size) for i in range(size)]
    return lax.ppermute(x, axis, pairs)


def taylor_constants():
    width = TIME_STEP / TICKS
    table = []
    for begin in range(TICKS):
        factorial = 1.0
        row = []
        for order in range(DERIVS):
            factorial = factorial * (order + 1)
            span = float((begin + 1) ** (order + 1) - begin ** (order + 1))
            row.append(span * width ** (order + 1) / factorial)
        table.append(row)
    return table


def low_half(shape, half):
    return lax.broadcasted_iota(jnp.int32, shape, len(shape) - 1) < half


def swap(x, half):
    return pltpu.roll(x, half, x.ndim - 1)


def pair(a, b):
    return jnp.concatenate([a, b], axis=-1)


def halves(x):
    high = x.astype(BF16).astype(F32)
    return high, x - high


def pad_rows(x, rows):
    if x.shape[0] == rows:
        return x
    return jnp.concatenate([x, jnp.zeros((rows - x.shape[0], x.shape[1]), x.dtype)], axis=0)


def timing(cluster, tick):
    period = jnp.where(cluster == 0, 4, jnp.where(cluster == 1, 2, 1))
    offset = jnp.where(cluster == 0, tick % 4, jnp.where(cluster == 1, tick % 2, 0))
    return offset, offset == period - 1


def right_operand(values):
    values = pad_rows(values, MODES_UP)
    high = values.astype(BF16)
    low = (values - high.astype(F32)).astype(BF16)
    return jnp.concatenate([high, high, low], axis=0)


def left_parts(matrix, up):
    rows = matrix.shape[0]
    if up > matrix.shape[1]:
        matrix = jnp.concatenate([matrix, jnp.zeros((rows, up - matrix.shape[1]), F32)], axis=1)
    high, low = halves(matrix)
    return jnp.concatenate([high, low, high], axis=1)


def send_choice(even, forward, backward):
    return jnp.where(even, forward, backward), jnp.where(even, backward, forward)


def parity(axis):
    if not paired(axis):
        return True, False
    even = lax.rem(lax.axis_index(axis), 2) == 0
    return even, even


def products(m_ref, slot, left, values, dirs, group, lanes):
    out = jnp.dot(left, right_operand(values), preferred_element_type=F32)
    if group == GROUPS[-1]:
        low = low_half((MODES, lanes), lanes // 2)
        for i in range(0, dirs, 2):
            one = out[i * MODES : (i + 1) * MODES]
            if i + 1 < dirs:
                one = jnp.where(low, one, out[(i + 1) * MODES : (i + 2) * MODES])
            m_ref[slot][-1][(i // 2) * MODES : (i // 2 + 1) * MODES, :] = one
    else:
        m_ref[slot][GROUPS.index(group)][...] = out


def contract(m_ref, slot, coef_ref, dirs, group, lanes):
    half = lanes // 2
    fields = [g for q in group for g in (2 * q, 2 * q + 1) if g < FIELDS]
    terms = [(d, q, q, d) for q in range(PAIRS - 1) for d in range(dirs)]
    terms += [(i, PAIRS - 1, PAIRS - 1, i) for i in range((dirs + 1) // 2)]
    columns = {q: [] for q in group}
    for row, count in BLOCKS:
        sums = {}
        for d, q, block, line in terms:
            at = (q % 2) * lanes
            values = m_ref[slot][q // 2][d * MODES + row : d * MODES + row + count, at : at + lanes]
            for g in fields:
                term = coef_ref[block * FIELDS + g, line : line + 1, :] * values
                sums[g] = sums[g] + term if g in sums else term
        low = low_half((count, lanes), half)
        for q in group:
            first = sums[2 * q]
            if 2 * q + 1 < FIELDS:
                second = sums[2 * q + 1]
                result = jnp.where(low, first, second) + swap(jnp.where(low, second, first), half)
            else:
                result = first + swap(first, half)
            columns[q].append(result)
    columns = [jnp.concatenate(columns[q], axis=0) for q in group]
    return columns[0] if len(columns) == 1 else jnp.concatenate(columns, axis=1)


def span(group, lanes):
    return slice(group[0] * lanes, (group[-1] + 1) * lanes)


def predict(state_of, ck_ref, star_ref, weight_ref, proj_ref, face_ref, m_ref, i_ref, lanes):
    def weight(order, group):
        row = weight_ref[order : order + 1, :]
        return row if len(group) == 1 else pair(row, row)

    for group in GROUPS:
        values = state_of(group)
        i_ref[:, span(group, lanes)] = weight(0, group) * values
        products(m_ref, 0, ck_ref[...], values, 3, group, lanes)
    for order in range(1, DERIVS):
        for group in GROUPS:
            values = contract(m_ref, (order - 1) % 2, star_ref, 3, group, lanes)
            total = i_ref[:, span(group, lanes)] + weight(order, group) * values
            i_ref[:, span(group, lanes)] = total
            if order < DERIVS - 1:
                products(m_ref, order % 2, ck_ref[...], values, 3, group, lanes)
            else:
                face_ref[:, span(group, lanes)] = jnp.dot(
                    proj_ref[...], right_operand(total), preferred_element_type=F32
                )


def store_weights(weight_ref, cluster, tick):
    offset, _ = timing(cluster, tick)
    table = taylor_constants()
    for order in range(DERIVS):
        row = jnp.full(cluster.shape, table[0][order], F32)
        for begin in range(1, TICKS):
            row = jnp.where(offset == begin, table[begin][order], row)
        weight_ref[order : order + 1, :] = row


def fill_table(face_ref, table_ref, lanes):
    half = lanes // 2
    low = low_half((FACE_UP, lanes), half)
    for q in range(PAIRS):
        for k in range(2):
            one = face_ref[2 * k * FACE_UP : (2 * k + 1) * FACE_UP, q * lanes : (q + 1) * lanes]
            two = face_ref[(2 * k + 1) * FACE_UP : (2 * k + 2) * FACE_UP, q * lanes : (q + 1) * lanes]
            crossed = swap(jnp.where(low, two, one), half)
            table_ref[2 * q * FACE_UP : (2 * q + 1) * FACE_UP, k * lanes : (k + 1) * lanes] = jnp.where(low, one, crossed)
            table_ref[(2 * q + 1) * FACE_UP : (2 * q + 2) * FACE_UP, k * lanes : (k + 1) * lanes] = jnp.where(
                low, crossed, two
            )


def pick(table, chosen):
    rows = table.shape[0]
    high, low = halves(table)
    both = jnp.concatenate([high, low], axis=0).astype(BF16)
    out = jnp.dot(both, chosen, preferred_element_type=F32)
    return out[:rows] + out[rows:]


def one_hot(index_row, rows):
    sub = lax.broadcasted_iota(jnp.int32, (rows, index_row.shape[1]), 0)
    return jnp.where(sub == index_row, 1.0, 0.0).astype(BF16)


def send_hot(index_row, lanes):
    half = lanes // 2
    column, _ = lane_places(1, lanes)
    sub = lax.broadcasted_iota(jnp.int32, (half, lanes), 0)
    blocks = []
    for j in range(4):
        for side in range(2):
            target = jnp.where(column % 2 == side, index_row - j * half, -1)
            blocks.append(jnp.where(sub == target, 1.0, 0.0).astype(BF16))
    return jnp.concatenate(blocks, axis=0)


def pick_faces(face_ref, chosen, lanes):
    rows = []
    for q in range(PAIRS):
        cols = slice(q * lanes, (q + 1) * lanes)
        rows.append(jnp.concatenate([face_ref[j * FACE_UP : (j + 1) * FACE_UP, cols] for j in range(4)], axis=1))
    return pick(jnp.concatenate(rows, axis=0), chosen)


def lane_places(rows, lanes):
    lane = lax.broadcasted_iota(jnp.int32, (rows, lanes), 1)
    return lane // (4 * SLOT), (lane // SLOT) % 4


def send_rows(face_ref, elem_ref, lanes):
    slots = face_ref.shape[1]
    half = lanes // 2
    index = face_ref[...] * half + elem_ref[...]
    index = jnp.concatenate([index] * (lanes // slots), axis=1)
    _, place = lane_places(1, lanes)
    rows = []
    for group in range(slots // SLOT):
        row = None
        for d in range(4):
            shift = ((d - group) * SLOT) % lanes
            moved = index[d : d + 1, :]
            moved = pltpu.roll(moved, shift, 1) if shift else moved
            row = moved if row is None else jnp.where(place == d, moved, row)
        rows.append(row)
    return rows


def fill_messages(picks, out_refs, lanes):
    column, place = lane_places(FACE_UP, lanes)
    for group, picked in enumerate(picks):
        pairs = [picked[q * FACE_UP : (q + 1) * FACE_UP] for q in range(PAIRS)]
        quads = [jnp.where(column < 2, pairs[0], pairs[1]), jnp.where(column < 2, pairs[2], pairs[3]), pairs[4]]
        messages = []
        for d in range(4):
            message = None
            for quad in range(3):
                shift = ((quad - d) * SLOT) % lanes
                moved = quads[quad] if shift == 0 else pltpu.roll(quads[quad], shift, 1)
                message = moved if message is None else jnp.where(place == quad, moved, message)
            messages.append(message)
        for axis, first in (("slab", 0), ("sub", 2)):
            even, _ = parity(axis)
            one, two = send_choice(even, messages[first], messages[first + 1])
            out_refs[first][group * FACE_UP : (group + 1) * FACE_UP, :] = one
            out_refs[first + 1][group * FACE_UP : (group + 1) * FACE_UP, :] = two


def face_operand(values):
    high, low = halves(values)
    return jnp.concatenate([high, high, low, jnp.zeros((SLOT, values.shape[1]), F32)], axis=0).astype(BF16)


def take_messages(in_refs, groups, far_ref, turn_ref, lanes):
    column, place = lane_places(FACE_UP, lanes)
    quads = []
    for group in range(groups):
        arrived = [ref[group * FACE_UP : (group + 1) * FACE_UP, :] for ref in in_refs]
        for axis, first in (("slab", 0), ("sub", 2)):
            _, even = parity(axis)
            arrived[first], arrived[first + 1] = send_choice(even, arrived[first + 1], arrived[first])
        for quad in range(3):
            merged = None
            for d in range(4):
                shift = ((d - quad) * SLOT) % lanes
                moved = arrived[d] if shift == 0 else pltpu.roll(arrived[d], shift, 1)
                merged = moved if merged is None else jnp.where(place == d, moved, merged)
            quads.append(merged)
    turned = jnp.dot(turn_ref[...], face_operand(jnp.concatenate(quads, axis=1)), preferred_element_type=F32)
    columns = []
    for group in range(groups):
        pieces = []
        for f in range(FIELDS):
            at = (3 * group + f // 4) * lanes
            piece = None
            for which in (2, 1, 0):
                moved = turned[which * FACE_UP : (which + 1) * FACE_UP, at : at + lanes]
                shift = ((which - f % 4) * 4 * SLOT) % lanes
                moved = pltpu.roll(moved, shift, 1) if shift else moved
                piece = moved if piece is None else jnp.where(column == which, moved, piece)
            pieces.append(piece)
        columns.append(jnp.concatenate(pieces, axis=0))
    left = columns[0] if groups == 1 else jnp.concatenate(columns, axis=1)
    return pick(left, far_ref[0 : groups * lanes, :])


def gather_faces(in_refs, groups, near_ref, far_ref, turn_ref, aplus_ref, c_ref, lanes):
    half = lanes // 2
    low = low_half((FACE_UP, lanes), half)
    values = near_ref[0 : FIELDS * FACE_UP, :] + take_messages(in_refs, groups, far_ref, turn_ref, lanes)
    for group in GROUPS:
        fields = [g for q in group for g in (2 * q, 2 * q + 1) if g < FIELDS]
        for k in range(2):
            sums = {}
            for f in range(FIELDS):
                part = values[f * FACE_UP : (f + 1) * FACE_UP, k * lanes : (k + 1) * lanes]
                for g in fields:
                    term = aplus_ref[f * FIELDS + g, k : k + 1, :] * part
                    sums[g] = sums[g] + term if g in sums else term
            for q in group:
                first = sums[2 * q]
                second = sums[min(2 * q + 1, FIELDS - 1)]
                crossed = swap(jnp.where(low, second, first), half)
                sides = jnp.concatenate([jnp.where(low, first, crossed), jnp.where(low, crossed, second)], axis=0)
                high = sides.astype(BF16)
                rest = (sides - high.astype(F32)).astype(BF16)
                at, cols = 2 * k * FACE_UP, slice(q * lanes, (q + 1) * lanes)
                c_ref[at : at + 2 * FACE_UP, cols] = high
                c_ref[4 * FACE_UP + at : 4 * FACE_UP + at + 2 * FACE_UP, cols] = high
                c_ref[8 * FACE_UP + at : 8 * FACE_UP + at + 2 * FACE_UP, cols] = rest


def updated(c_ref, lift_ref, base_ref, finished, group, lanes):
    cols = span(group, lanes)
    outer = jnp.dot(lift_ref[...], c_ref[:, cols], preferred_element_type=F32)
    before = base_ref[:, cols]
    done = finished if len(group) == 1 else jnp.concatenate([finished, finished], axis=1)
    return jnp.where(done, before - outer, before)


def pack_coefs(ref, dirs, base, out_ref):
    for q in range(PAIRS - 1):
        for g in range(FIELDS):
            out_ref[q * FIELDS + g, base : base + dirs, :] = pair(ref[2 * q, g], ref[2 * q + 1, g])


def pack_last(lines, g, out_ref):
    for i in range(0, len(lines), 2):
        other = lines[i + 1] if i + 1 < len(lines) else jnp.zeros_like(lines[i])
        out_ref[(PAIRS - 1) * FIELDS + g, i // 2 : i // 2 + 1, :] = pair(lines[i], other)


def first_kernel(
    state_hbm, star_hbm, ck_hbm, project_hbm, cluster_hbm, elem_hbm, face_hbm, *rest, lanes
):
    count = (len(rest) - 14) // 2
    late_hbm, rest = rest[:count], rest[count:]
    packed_ref, star_out, ck_out, proj_out, send_out, star_ref, cluster_ref = rest[:7]
    late_out, rest = rest[7 : 7 + count], rest[7 + count :]
    state_ref, ck_ref, project_ref, elem_ref, face_ref, early, late = rest
    soon = [
        pltpu.make_async_copy(source, target, early.at[i])
        for i, (source, target) in enumerate((
            (star_hbm, star_ref), (state_hbm, state_ref), (ck_hbm, ck_ref), (project_hbm, project_ref),
            (elem_hbm, elem_ref), (face_hbm, face_ref), (cluster_hbm, cluster_ref),
        ))
    ]
    then = [pltpu.make_async_copy(a, b, late.at[i]) for i, (a, b) in enumerate(zip(late_hbm, late_out))]
    for copy in soon + then:
        copy.start()
    soon[0].wait()
    pack_coefs(star_ref, 3, 0, star_out)
    for g in range(FIELDS):
        both = star_ref[FIELDS - 1, g]
        pack_last([both[d : d + 1] for d in range(3)], g, star_out)
    soon[1].wait()
    for q in range(PAIRS):
        packed_ref[:, q * lanes : (q + 1) * lanes] = pair(state_ref[2 * q], state_ref[min(2 * q + 1, FIELDS - 1)])
    for copy in soon[2:]:
        copy.wait()
    ck_out[...] = left_parts(-ck_ref[...].reshape(3 * MODES, MODES), MODES_UP).astype(BF16)
    proj_rows = [pad_rows(project_ref[:, j, :], FACE_UP) for j in range(4)]
    proj_out[...] = left_parts(jnp.concatenate(proj_rows, axis=0), MODES_UP).astype(BF16)
    for i, row in enumerate(send_rows(face_ref, elem_ref, lanes)):
        send_out[i : i + 1, :] = row
    for copy in then:
        copy.wait()


def predict_kernel(
    packed_ref, cluster_ref, ck_ref, star_ref, proj_ref, i_ref, faces_ref, weight_ref, m_ref, *, lanes, tick
):
    store_weights(weight_ref, pair(cluster_ref[...], cluster_ref[...]), tick)

    def state_of(group):
        return packed_ref[:, span(group, lanes)]

    predict(state_of, ck_ref, star_ref, weight_ref, proj_ref, faces_ref, m_ref, i_ref, lanes)


def send_kernel(faces_ref, send_ref, *rest, lanes, tick):
    if tick % 2:
        held_ref, rest = rest[0], rest[1:]
    count = GROUPS_AT[tick]
    chosen = send_ref[:, 0 : count * lanes] if tick else send_hot(send_ref[0:1, :], lanes)
    picked = pick_faces(faces_ref, chosen, lanes)
    picks = [picked[:, group * lanes : (group + 1) * lanes] for group in range(count)]
    for group in range(1, count):
        picks[group] = picks[group] + held_ref[:, (group - 1) * lanes : group * lanes]
    fill_messages(picks, rest, lanes)


def prepare_kernel(
    star_ref, aminus_ref, aplus_ref, vol_ref, flux_ref, lift_ref, rotate_ref, neighbour_ref, orient_ref, send_ref,
    coef_out, aplus_out, left_out, lift_out, turn_out, near_out, far_out, send_out, *, lanes,
):
    half = lanes // 2
    pack_coefs(star_ref, 3, 0, coef_out)
    pack_coefs(aminus_ref, 4, 3, coef_out)
    for g in range(FIELDS):
        ahead, behind = star_ref[FIELDS - 1, g], aminus_ref[FIELDS - 1, g]
        pack_last([ahead[d : d + 1] for d in range(3)] + [behind[j : j + 1] for j in range(4)], g, coef_out)
        for f in range(FIELDS):
            own = aplus_ref[f, g]
            for k in range(2):
                aplus_out[f * FIELDS + g, k : k + 1, :] = pair(own[2 * k : 2 * k + 1], own[2 * k + 1 : 2 * k + 2])
    both = jnp.concatenate([vol_ref[...].reshape(3 * MODES, MODES), -flux_ref[...].reshape(4 * MODES, MODES)], axis=0)
    left_out[...] = left_parts(both, MODES_UP).astype(BF16)
    lift = jnp.concatenate([pad_rows(lift_ref[:, j, :], FACE_UP) for j in range(4)], axis=0)
    lift = jnp.concatenate([lift, jnp.zeros((4 * FACE_UP, lanes - MODES), F32)], axis=1)
    lift = jnp.transpose(pad_rows(lift, lanes))[0:MODES, 0 : 4 * FACE_UP]
    lift_out[...] = left_parts(lift, 4 * FACE_UP).astype(BF16)
    turns = jnp.concatenate([pad_rows(rotate_ref[which], FACE_UP) for which in range(3)], axis=0)
    turn_out[...] = jnp.concatenate([left_parts(turns, FACE_UP), jnp.zeros((3 * FACE_UP, SLOT), F32)], axis=1).astype(BF16)
    row = jnp.concatenate([neighbour_ref[j : j + 1, :] for j in range(4)], axis=1)
    turned = jnp.concatenate([orient_ref[j : j + 1, :] for j in range(4)], axis=1)
    near_out[...] = one_hot(row, 4 * half)
    sub = lax.broadcasted_iota(jnp.int32, (lanes, 4 * half), 0)
    for group in range(send_ref.shape[0]):
        target = 4 * half + ((sub // SLOT) % 4) * (4 * SLOT) + group * SLOT + sub % SLOT
        hit = (target == row) & (turned == sub // (4 * SLOT))
        far_out[group * lanes : (group + 1) * lanes, :] = jnp.where(hit, 1.0, 0.0).astype(BF16)
    for group in range(send_ref.shape[0]):
        send_out[:, group * lanes : (group + 1) * lanes] = send_hot(send_ref[group : group + 1, :], lanes)


def local_kernel(
    i_ref, packed_ref, faces_ref, cluster_ref, coef_ref, left_ref, near_ref, turn_ref, orient_ref, own_ref, seen_ref,
    send_ref, held_ref, base_out, own_out, seen_out, *rest, lanes, tick,
):
    m_ref, table_ref = rest[-2:]
    fill_table(faces_ref, table_ref, lanes)
    if tick < TICKS - 1:
        picked = pick_faces(faces_ref, send_ref[:, lanes:], lanes)
        rest[0][:, 0:lanes] = picked[:, 0:lanes]
        rest[0][:, lanes:] = held_ref[:, lanes:] + picked[:, lanes:] if tick else picked[:, lanes:]
    cluster = pair(cluster_ref[...], cluster_ref[...])
    offset, finished = timing(cluster, tick)
    two = jnp.concatenate([offset, offset], axis=1)
    for group in GROUPS:
        cols = span(group, lanes)
        values = i_ref[:, cols]
        if tick:
            fresh = (offset if len(group) == 1 else two) == 0
            values = jnp.where(fresh, values, own_ref[:, cols] + values)
        own_out[:, cols] = values
        products(m_ref, 0, left_ref[...], values, 7, group, lanes)
    seen = pick(table_ref[...], near_ref[...])
    which = jnp.concatenate([orient_ref[j : j + 1, :] for j in range(4)], axis=1)
    for f in range(FIELDS):
        rows = slice(f * FACE_UP, (f + 1) * FACE_UP)
        turned = jnp.dot(turn_ref[...], face_operand(seen[rows]), preferred_element_type=F32)
        part = jnp.where(
            which == 0,
            turned[0:FACE_UP],
            jnp.where(which == 1, turned[FACE_UP : 2 * FACE_UP], turned[2 * FACE_UP : 3 * FACE_UP]),
        )
        seen_out[rows, :] = jnp.where(two == 0, part, seen_ref[rows, :] + part) if tick else part
    seen_out[FIELDS * FACE_UP :, :] = jnp.zeros((ROWS - FIELDS * FACE_UP, 2 * lanes), F32)
    for group in GROUPS:
        cols = span(group, lanes)
        before = packed_ref[:, cols]
        change = contract(m_ref, 0, coef_ref, 7, group, lanes)
        done = finished if len(group) == 1 else jnp.concatenate([finished, finished], axis=1)
        base_out[:, cols] = jnp.where(done, before + change, before)


def update_kernel(
    r0, r1, r2, r3, near_ref, far_ref, turn_ref, aplus_ref, lift_ref, base_ref, cluster_ref, packed_ref, c_ref,
    *, lanes, tick, groups,
):
    _, finished = timing(pair(cluster_ref[...], cluster_ref[...]), tick)
    gather_faces((r0, r1, r2, r3), groups, near_ref, far_ref, turn_ref, aplus_ref, c_ref, lanes)
    for group in GROUPS:
        packed_ref[:, span(group, lanes)] = updated(c_ref, lift_ref, base_ref, finished, group, lanes)


def last_kernel(
    r0, r1, r2, r3, near_ref, far_ref, turn_ref, aplus_ref, lift_ref, base_ref, cluster_ref, result_hbm,
    c_ref, out_ref, gone, *, lanes,
):
    half = lanes // 2
    copies = []
    _, finished = timing(pair(cluster_ref[...], cluster_ref[...]), TICKS - 1)
    gather_faces((r0, r1, r2, r3), 4, near_ref, far_ref, turn_ref, aplus_ref, c_ref, lanes)
    for group in GROUPS:
        values = updated(c_ref, lift_ref, base_ref, finished, group, lanes)
        for i, q in enumerate(group):
            for side in range(2):
                if 2 * q + side < FIELDS:
                    out_ref[2 * q + side] = values[:, i * lanes + side * half : i * lanes + (side + 1) * half]
        fields = pl.ds(2 * group[0], min(2 * len(group), FIELDS - 2 * group[0]))
        copy = pltpu.make_async_copy(out_ref.at[fields], result_hbm.at[fields], gone.at[GROUPS.index(group)])
        copy.start()
        copies.append(copy)
    for copy in copies:
        copy.wait()


def stages(slots, dirs, lanes):
    wide = pltpu.VMEM((dirs * MODES, 2 * lanes), F32)
    last = pltpu.VMEM(((dirs + 1) // 2 * MODES, lanes), F32)
    return [[wide, wide, last] for _ in range(slots)]


def call(body, outs, scratch, name, flops, arrays, far=0, far_out=False):
    moved = sum(a.size * a.dtype.itemsize for a in arrays)
    hbm = pltpu.MemorySpace.HBM
    near = len(arrays) - far
    arrays = [*arrays[:near], *(pltpu.with_memory_space_constraint(x, hbm) for x in arrays[near:])]
    spaces = [pltpu.VMEM] * near + [hbm] * far
    return pl.pallas_call(
        body,
        out_shape=outs,
        in_specs=[pl.BlockSpec(memory_space=space) for space in spaces],
        out_specs=[pl.BlockSpec(memory_space=hbm if far_out else pltpu.VMEM)] * len(outs),
        scratch_shapes=scratch,
        compiler_params=pltpu.CompilerParams(vmem_limit_bytes=24 << 20),
        cost_estimate=pl.CostEstimate(flops=flops, bytes_accessed=moved, transcendentals=0),
        name=name,
    )(*arrays)


def shards(
    state, star, aminus, aplus, ck_stiff, vol_stiff, flux_local, lift, rotate, project,
    cluster, orient, neighbour, send_elem, send_face,
):
    elems = state.shape[-1]
    lanes = 2 * elems
    wide = PAIRS * lanes
    groups = send_elem.shape[1] // SLOT
    shape = jax.ShapeDtypeStruct
    cluster_row = cluster.reshape(1, elems)
    star, aminus, aplus = (jnp.transpose(x, (1, 2, 0, 3)) for x in (star, aminus, aplus))
    project = jnp.transpose(project, (1, 0, 2))
    lift = jnp.transpose(lift, (2, 0, 1))

    modal = shape((MODES, wide), F32)
    table = shape((ROWS, 4 * elems), F32)
    weights = pltpu.VMEM((SLOT, lanes), F32)
    faces = shape((4 * FACE_UP, wide), F32)
    staged = stages(2, 3, lanes)
    sides = pltpu.VMEM((12 * FACE_UP, wide), BF16)

    def like(x):
        return shape(x.shape, x.dtype)

    def room(x):
        return pltpu.VMEM(x.shape, x.dtype)

    def message(count):
        return [shape((count * FACE_UP, lanes), F32)] * 4

    late = (aminus, aplus, vol_stiff, flux_local, lift, rotate, neighbour, orient)
    packed, star_pairs, ck_left, proj_left, send, star, cluster_row, *late = call(
        functools.partial(first_kernel, lanes=lanes),
        [
            modal,
            shape((PAIRS * FIELDS, 3, lanes), F32),
            shape((3 * MODES, 3 * MODES_UP), BF16),
            shape((4 * FACE_UP, 3 * MODES_UP), BF16),
            shape((groups, lanes), jnp.int32),
            like(star),
            like(cluster_row),
        ]
        + [like(x) for x in late],
        [room(state), room(ck_stiff), room(project), room(send_elem), room(send_face)]
        + [pltpu.SemaphoreType.DMA((7,)), pltpu.SemaphoreType.DMA((len(late),))],
        "first", 10_000_000,
        (state, star, ck_stiff, project, cluster_row, send_elem, send_face, *late), far=7 + len(late),
    )
    orient = late[-1]

    def predicted(tick, packed, chosen, more):
        integral, face_values = call(
            functools.partial(predict_kernel, lanes=lanes, tick=tick),
            [modal, faces],
            [weights, staged],
            f"predict{tick}", 400_000_000,
            (packed, cluster_row, ck_left, star_pairs, proj_left),
        )
        messages = call(
            functools.partial(send_kernel, lanes=lanes, tick=tick),
            message(GROUPS_AT[tick]), [], f"send{tick}", 50_000_000, (face_values, chosen, *more),
        )
        return integral, face_values, messages

    integral, face_values, messages = predicted(0, packed, send, ())
    coef, aplus_pairs, left, lift_left, turn, near_hot, far_hot, chosen = call(
        functools.partial(prepare_kernel, lanes=lanes),
        [
            shape((PAIRS * FIELDS, 7, lanes), F32),
            shape((FIELDS * FIELDS, 2, lanes), F32),
            shape((7 * MODES, 3 * MODES_UP), BF16),
            shape((MODES, 12 * FACE_UP), BF16),
            shape((3 * FACE_UP, 80), BF16),
            shape((4 * elems, 4 * elems), BF16),
            shape((groups * lanes, 4 * elems), BF16),
            shape((4 * lanes, groups * lanes), BF16),
        ],
        [],
        "prepare", 100_000_000,
        (star, *late, send),
    )
    own = integral
    seen = near_hot
    held = near_hot
    for tick in range(TICKS):
        arrived = [None] * 4
        for slot, axis, phase in ((1, "slab", 1), (0, "slab", 0), (3, "sub", 1), (2, "sub", 0)):
            arrived[slot] = exchange(messages[slot], axis, phase)
        last = tick == TICKS - 1
        base, own, seen, *kept = call(
            functools.partial(local_kernel, lanes=lanes, tick=tick),
            [modal, modal, table] + ([] if last else [shape((PAIRS * FACE_UP, (groups - 1) * lanes), F32)]),
            [stages(1, 7, lanes), pltpu.VMEM((ROWS, 4 * elems), F32)],
            f"local{tick}", 300_000_000,
            (integral, packed, face_values, cluster_row, coef, left, near_hot, turn, orient, own, seen, chosen, held),
        )
        held = held if last else kept[0]
        count = GROUPS_AT[tick]
        common = (*arrived, seen, far_hot, turn, aplus_pairs, lift_left, base, cluster_row)
        if last:
            return call(
                functools.partial(last_kernel, lanes=lanes),
                [shape(state.shape, F32)],
                [sides, room(state), pltpu.SemaphoreType.DMA((len(GROUPS),))],
                "last", 100_000_000, common, far_out=True,
            )[0]
        packed = call(
            functools.partial(update_kernel, lanes=lanes, tick=tick, groups=count),
            [modal],
            [sides],
            f"update{tick}", 100_000_000, common,
        )[0]
        integral, face_values, messages = predicted(tick + 1, packed, chosen, (held,) if tick % 2 == 0 else ())


def solution(mesh):
    placed = (
        P(None, None, ("slab", "sub")),
        P(None, None, None, ("slab", "sub")),
        P(None, None, None, ("slab", "sub")),
        P(None, None, None, ("slab", "sub")),
        P(),
        P(),
        P(),
        P(),
        P(),
        P(),
        P(("slab", "sub")),
        P(None, ("slab", "sub")),
        P(None, ("slab", "sub")),
        P(None, ("slab", "sub")),
        P(None, ("slab", "sub")),
    )
    return jax.shard_map(
        shards,
        mesh=mesh,
        in_specs=placed,
        out_specs=P(None, None, ("slab", "sub")),
        check_vma=False,
    )
```

```python
import functools

import jax
import jax.numpy as jnp
from jax import lax
from jax.experimental import pallas as pl
from jax.experimental.pallas import tpu as pltpu
from jax.sharding import PartitionSpec as P

FIELDS = 9
PAIRS = 5
MODES = 56
MODES_UP = 64
FACE_MODES = 21
FACE_UP = 24
ROWS = 2 * PAIRS * FACE_UP
DERIVS = 6
TICKS = 4
SLOT = 8
TIME_STEP = 1.0
F32 = jnp.float32
BF16 = jnp.bfloat16
BLOCKS = ((0, 32), (32, 24))
GROUPS = ((0, 1), (2, 3), (4,))
GROUPS_AT = (1, 2, 1, 4)


def paired(axis):
    return lax.axis_size(axis) % 2 == 0


def exchange(x, axis, phase):
    size = lax.axis_size(axis)
    if paired(axis):
        pairs = []
        for i in range(phase, size + phase, 2):
            one, two = i % size, (i + 1) % size
            pairs += [(one, two), (two, one)]
    else:
        by = 1 if phase == 0 else -1
        pairs = [(i, (i + by) % size) for i in range(size)]
    return lax.ppermute(x, axis, pairs)


def taylor_constants():
    width = TIME_STEP / TICKS
    table = []
    for begin in range(TICKS):
        factorial = 1.0
        row = []
        for order in range(DERIVS):
            factorial = factorial * (order + 1)
            span = float((begin + 1) ** (order + 1) - begin ** (order + 1))
            row.append(span * width ** (order + 1) / factorial)
        table.append(row)
    return table


def low_half(shape, half):
    return lax.broadcasted_iota(jnp.int32, shape, len(shape) - 1) < half


def swap(x, half):
    return pltpu.roll(x, half, x.ndim - 1)


def pair(a, b):
    return jnp.concatenate([a, b], axis=-1)


def halves(x):
    high = x.astype(BF16).astype(F32)
    return high, x - high


def pad_rows(x, rows):
    if x.shape[0] == rows:
        return x
    return jnp.concatenate([x, jnp.zeros((rows - x.shape[0], x.shape[1]), x.dtype)], axis=0)


def timing(cluster, tick):
    period = jnp.where(cluster == 0, 4, jnp.where(cluster == 1, 2, 1))
    offset = jnp.where(cluster == 0, tick % 4, jnp.where(cluster == 1, tick % 2, 0))
    return offset, offset == period - 1


def right_operand(values):
    values = pad_rows(values, MODES_UP)
    high = values.astype(BF16)
    low = (values - high.astype(F32)).astype(BF16)
    return jnp.concatenate([high, high, low], axis=0)


def left_parts(matrix, up):
    rows = matrix.shape[0]
    if up > matrix.shape[1]:
        matrix = jnp.concatenate([matrix, jnp.zeros((rows, up - matrix.shape[1]), F32)], axis=1)
    high, low = halves(matrix)
    return jnp.concatenate([high, low, high], axis=1)


def send_choice(even, forward, backward):
    return jnp.where(even, forward, backward), jnp.where(even, backward, forward)


def parity(axis):
    if not paired(axis):
        return True, False
    even = lax.rem(lax.axis_index(axis), 2) == 0
    return even, even


def products(m_ref, slot, left, values, dirs, group, lanes):
    out = jnp.dot(left, right_operand(values), preferred_element_type=F32)
    if group == GROUPS[-1]:
        low = low_half((MODES, lanes), lanes // 2)
        for i in range(0, dirs, 2):
            one = out[i * MODES : (i + 1) * MODES]
            if i + 1 < dirs:
                one = jnp.where(low, one, out[(i + 1) * MODES : (i + 2) * MODES])
            m_ref[slot][-1][(i // 2) * MODES : (i // 2 + 1) * MODES, :] = one
    else:
        m_ref[slot][GROUPS.index(group)][...] = out


def contract(m_ref, slot, coef_ref, dirs, group, lanes):
    half = lanes // 2
    fields = [g for q in group for g in (2 * q, 2 * q + 1) if g < FIELDS]
    terms = [(d, q, q, d) for q in range(PAIRS - 1) for d in range(dirs)]
    terms += [(i, PAIRS - 1, PAIRS - 1, i) for i in range((dirs + 1) // 2)]
    columns = {q: [] for q in group}
    for row, count in BLOCKS:
        sums = {}
        for d, q, block, line in terms:
            at = (q % 2) * lanes
            values = m_ref[slot][q // 2][d * MODES + row : d * MODES + row + count, at : at + lanes]
            for g in fields:
                term = coef_ref[block * FIELDS + g, line : line + 1, :] * values
                sums[g] = sums[g] + term if g in sums else term
        low = low_half((count, lanes), half)
        for q in group:
            first = sums[2 * q]
            if 2 * q + 1 < FIELDS:
                second = sums[2 * q + 1]
                result = jnp.where(low, first, second) + swap(jnp.where(low, second, first), half)
            else:
                result = first + swap(first, half)
            columns[q].append(result)
    columns = [jnp.concatenate(columns[q], axis=0) for q in group]
    return columns[0] if len(columns) == 1 else jnp.concatenate(columns, axis=1)


def span(group, lanes):
    return slice(group[0] * lanes, (group[-1] + 1) * lanes)


def predict(state_of, ck_ref, star_ref, weight_ref, proj_ref, face_ref, m_ref, i_ref, lanes):
    def weight(order, group):
        row = weight_ref[order : order + 1, :]
        return row if len(group) == 1 else pair(row, row)

    for group in GROUPS:
        values = state_of(group)
        i_ref[:, span(group, lanes)] = weight(0, group) * values
        products(m_ref, 0, ck_ref[...], values, 3, group, lanes)
    for order in range(1, DERIVS):
        for group in GROUPS:
            values = contract(m_ref, (order - 1) % 2, star_ref, 3, group, lanes)
            total = i_ref[:, span(group, lanes)] + weight(order, group) * values
            i_ref[:, span(group, lanes)] = total
            if order < DERIVS - 1:
                products(m_ref, order % 2, ck_ref[...], values, 3, group, lanes)
            else:
                face_ref[:, span(group, lanes)] = jnp.dot(
                    proj_ref[...], right_operand(total), preferred_element_type=F32
                )


def store_weights(weight_ref, cluster, tick):
    offset, _ = timing(cluster, tick)
    table = taylor_constants()
    for order in range(DERIVS):
        row = jnp.full(cluster.shape, table[0][order], F32)
        for begin in range(1, TICKS):
            row = jnp.where(offset == begin, table[begin][order], row)
        weight_ref[order : order + 1, :] = row


def fill_table(face_ref, table_ref, lanes):
    half = lanes // 2
    low = low_half((FACE_UP, lanes), half)
    for q in range(PAIRS):
        for k in range(2):
            one = face_ref[2 * k * FACE_UP : (2 * k + 1) * FACE_UP, q * lanes : (q + 1) * lanes]
            two = face_ref[(2 * k + 1) * FACE_UP : (2 * k + 2) * FACE_UP, q * lanes : (q + 1) * lanes]
            crossed = swap(jnp.where(low, two, one), half)
            table_ref[2 * q * FACE_UP : (2 * q + 1) * FACE_UP, k * lanes : (k + 1) * lanes] = jnp.where(low, one, crossed)
            table_ref[(2 * q + 1) * FACE_UP : (2 * q + 2) * FACE_UP, k * lanes : (k + 1) * lanes] = jnp.where(
                low, crossed, two
            )


def pick(table, chosen):
    rows = table.shape[0]
    high, low = halves(table)
    both = jnp.concatenate([high, low], axis=0).astype(BF16)
    out = jnp.dot(both, chosen, preferred_element_type=F32)
    return out[:rows] + out[rows:]


def one_hot(index_row, rows):
    sub = lax.broadcasted_iota(jnp.int32, (rows, index_row.shape[1]), 0)
    return jnp.where(sub == index_row, 1.0, 0.0).astype(BF16)


def send_hot(index_row, lanes):
    half = lanes // 2
    column, _ = lane_places(1, lanes)
    sub = lax.broadcasted_iota(jnp.int32, (half, lanes), 0)
    blocks = []
    for j in range(4):
        for side in range(2):
            target = jnp.where(column % 2 == side, index_row - j * half, -1)
            blocks.append(jnp.where(sub == target, 1.0, 0.0).astype(BF16))
    return jnp.concatenate(blocks, axis=0)


def pick_faces(face_ref, chosen, lanes):
    rows = []
    for q in range(PAIRS):
        cols = slice(q * lanes, (q + 1) * lanes)
        rows.append(jnp.concatenate([face_ref[j * FACE_UP : (j + 1) * FACE_UP, cols] for j in range(4)], axis=1))
    return pick(jnp.concatenate(rows, axis=0), chosen)


def lane_places(rows, lanes):
    lane = lax.broadcasted_iota(jnp.int32, (rows, lanes), 1)
    return lane // (4 * SLOT), (lane // SLOT) % 4


def send_rows(face_ref, elem_ref, lanes):
    slots = face_ref.shape[1]
    half = lanes // 2
    index = face_ref[...] * half + elem_ref[...]
    index = jnp.concatenate([index] * (lanes // slots), axis=1)
    _, place = lane_places(1, lanes)
    rows = []
    for group in range(slots // SLOT):
        row = None
        for d in range(4):
            shift = ((d - group) * SLOT) % lanes
            moved = index[d : d + 1, :]
            moved = pltpu.roll(moved, shift, 1) if shift else moved
            row = moved if row is None else jnp.where(place == d, moved, row)
        rows.append(row)
    return rows


def fill_messages(picks, out_refs, lanes):
    column, place = lane_places(FACE_UP, lanes)
    for group, picked in enumerate(picks):
        pairs = [picked[q * FACE_UP : (q + 1) * FACE_UP] for q in range(PAIRS)]
        quads = [jnp.where(column < 2, pairs[0], pairs[1]), jnp.where(column < 2, pairs[2], pairs[3]), pairs[4]]
        messages = []
        for d in range(4):
            message = None
            for quad in range(3):
                shift = ((quad - d) * SLOT) % lanes
                moved = quads[quad] if shift == 0 else pltpu.roll(quads[quad], shift, 1)
                message = moved if message is None else jnp.where(place == quad, moved, message)
            messages.append(message)
        for axis, first in (("slab", 0), ("sub", 2)):
            even, _ = parity(axis)
            one, two = send_choice(even, messages[first], messages[first + 1])
            out_refs[first][group * FACE_UP : (group + 1) * FACE_UP, :] = one
            out_refs[first + 1][group * FACE_UP : (group + 1) * FACE_UP, :] = two


def face_operand(values):
    high, low = halves(values)
    return jnp.concatenate([high, high, low, jnp.zeros((SLOT, values.shape[1]), F32)], axis=0).astype(BF16)


def take_messages(in_refs, groups, far_ref, turn_ref, lanes):
    column, place = lane_places(FACE_UP, lanes)
    quads = []
    for group in range(groups):
        arrived = [ref[group * FACE_UP : (group + 1) * FACE_UP, :] for ref in in_refs]
        for axis, first in (("slab", 0), ("sub", 2)):
            _, even = parity(axis)
            arrived[first], arrived[first + 1] = send_choice(even, arrived[first + 1], arrived[first])
        for quad in range(3):
            merged = None
            for d in range(4):
                shift = ((d - quad) * SLOT) % lanes
                moved = arrived[d] if shift == 0 else pltpu.roll(arrived[d], shift, 1)
                merged = moved if merged is None else jnp.where(place == d, moved, merged)
            quads.append(merged)
    turned = jnp.dot(turn_ref[...], face_operand(jnp.concatenate(quads, axis=1)), preferred_element_type=F32)
    columns = []
    for group in range(groups):
        pieces = []
        for f in range(FIELDS):
            at = (3 * group + f // 4) * lanes
            piece = None
            for which in (2, 1, 0):
                moved = turned[which * FACE_UP : (which + 1) * FACE_UP, at : at + lanes]
                shift = ((which - f % 4) * 4 * SLOT) % lanes
                moved = pltpu.roll(moved, shift, 1) if shift else moved
                piece = moved if piece is None else jnp.where(column == which, moved, piece)
            pieces.append(piece)
        columns.append(jnp.concatenate(pieces, axis=0))
    left = columns[0] if groups == 1 else jnp.concatenate(columns, axis=1)
    chosen = far_ref[0 : groups * lanes, :]
    if groups > 1:
        return pick(left, chosen)
    high, low = halves(left)
    both = jnp.concatenate([high, low], axis=1).astype(BF16)
    return jnp.dot(both, jnp.concatenate([chosen, chosen], axis=0), preferred_element_type=F32)


def gather_faces(in_refs, groups, near_ref, far_ref, turn_ref, aplus_ref, c_ref, lanes):
    half = lanes // 2
    low = low_half((FACE_UP, lanes), half)
    values = near_ref[0 : FIELDS * FACE_UP, :] + take_messages(in_refs, groups, far_ref, turn_ref, lanes)
    for group in GROUPS:
        fields = [g for q in group for g in (2 * q, 2 * q + 1) if g < FIELDS]
        for k in range(2):
            sums = {}
            for f in range(FIELDS):
                part = values[f * FACE_UP : (f + 1) * FACE_UP, k * lanes : (k + 1) * lanes]
                for g in fields:
                    term = aplus_ref[f * FIELDS + g, k : k + 1, :] * part
                    sums[g] = sums[g] + term if g in sums else term
            for q in group:
                first = sums[2 * q]
                second = sums[min(2 * q + 1, FIELDS - 1)]
                crossed = swap(jnp.where(low, second, first), half)
                sides = jnp.concatenate([jnp.where(low, first, crossed), jnp.where(low, crossed, second)], axis=0)
                high = sides.astype(BF16)
                rest = (sides - high.astype(F32)).astype(BF16)
                at, cols = 2 * k * FACE_UP, slice(q * lanes, (q + 1) * lanes)
                c_ref[at : at + 2 * FACE_UP, cols] = high
                c_ref[4 * FACE_UP + at : 4 * FACE_UP + at + 2 * FACE_UP, cols] = high
                c_ref[8 * FACE_UP + at : 8 * FACE_UP + at + 2 * FACE_UP, cols] = rest


def updated(c_ref, lift_ref, base_ref, finished, group, lanes):
    cols = span(group, lanes)
    outer = jnp.dot(lift_ref[...], c_ref[:, cols], preferred_element_type=F32)
    before = base_ref[:, cols]
    done = finished if len(group) == 1 else jnp.concatenate([finished, finished], axis=1)
    return jnp.where(done, before - outer, before)


def pack_coefs(ref, dirs, base, out_ref):
    for q in range(PAIRS - 1):
        for g in range(FIELDS):
            out_ref[q * FIELDS + g, base : base + dirs, :] = pair(ref[2 * q, g], ref[2 * q + 1, g])


def pack_last(lines, g, out_ref):
    for i in range(0, len(lines), 2):
        other = lines[i + 1] if i + 1 < len(lines) else jnp.zeros_like(lines[i])
        out_ref[(PAIRS - 1) * FIELDS + g, i // 2 : i // 2 + 1, :] = pair(lines[i], other)


def first_kernel(
    state_hbm, star_hbm, ck_hbm, project_hbm, cluster_hbm, elem_hbm, face_hbm, *rest, lanes
):
    count = (len(rest) - 14) // 2
    late_hbm, rest = rest[:count], rest[count:]
    packed_ref, star_out, ck_out, proj_out, send_out, star_ref, cluster_ref = rest[:7]
    late_out, rest = rest[7 : 7 + count], rest[7 + count :]
    state_ref, ck_ref, project_ref, elem_ref, face_ref, early, late = rest
    soon = [
        pltpu.make_async_copy(source, target, early.at[i])
        for i, (source, target) in enumerate((
            (star_hbm, star_ref), (state_hbm, state_ref), (ck_hbm, ck_ref), (project_hbm, project_ref),
            (elem_hbm, elem_ref), (face_hbm, face_ref), (cluster_hbm, cluster_ref),
        ))
    ]
    then = [pltpu.make_async_copy(a, b, late.at[i]) for i, (a, b) in enumerate(zip(late_hbm, late_out))]
    for copy in soon + then:
        copy.start()
    soon[0].wait()
    pack_coefs(star_ref, 3, 0, star_out)
    for g in range(FIELDS):
        both = star_ref[FIELDS - 1, g]
        pack_last([both[d : d + 1] for d in range(3)], g, star_out)
    soon[1].wait()
    for q in range(PAIRS):
        packed_ref[:, q * lanes : (q + 1) * lanes] = pair(state_ref[2 * q], state_ref[min(2 * q + 1, FIELDS - 1)])
    for copy in soon[2:]:
        copy.wait()
    ck_out[...] = left_parts(-ck_ref[...].reshape(3 * MODES, MODES), MODES_UP).astype(BF16)
    proj_rows = [pad_rows(project_ref[:, j, :], FACE_UP) for j in range(4)]
    proj_out[...] = left_parts(jnp.concatenate(proj_rows, axis=0), MODES_UP).astype(BF16)
    for i, row in enumerate(send_rows(face_ref, elem_ref, lanes)):
        send_out[i : i + 1, :] = row
    for copy in then:
        copy.wait()


def predict_kernel(
    packed_ref, cluster_ref, ck_ref, star_ref, proj_ref, i_ref, faces_ref, weight_ref, m_ref, *, lanes, tick
):
    store_weights(weight_ref, pair(cluster_ref[...], cluster_ref[...]), tick)

    def state_of(group):
        return packed_ref[:, span(group, lanes)]

    predict(state_of, ck_ref, star_ref, weight_ref, proj_ref, faces_ref, m_ref, i_ref, lanes)


def send_kernel(faces_ref, send_ref, *rest, lanes, tick):
    if tick % 2:
        held_ref, rest = rest[0], rest[1:]
    count = GROUPS_AT[tick]
    chosen = send_ref[:, 0 : count * lanes] if tick else send_hot(send_ref[0:1, :], lanes)
    picked = pick_faces(faces_ref, chosen, lanes)
    picks = [picked[:, group * lanes : (group + 1) * lanes] for group in range(count)]
    for group in range(1, count):
        picks[group] = picks[group] + held_ref[:, (group - 1) * lanes : group * lanes]
    fill_messages(picks, rest, lanes)


def predict_send_kernel(packed_ref, cluster_ref, ck_ref, star_ref, proj_ref, send_ref, *rest, lanes, tick):
    held = rest[:1] if tick % 2 else ()
    i_ref, faces_ref, *outs = rest[len(held) : len(held) + 6]
    weight_ref, m_ref = rest[len(held) + 6 :]
    predict_kernel(
        packed_ref, cluster_ref, ck_ref, star_ref, proj_ref, i_ref, faces_ref, weight_ref, m_ref, lanes=lanes, tick=tick
    )
    send_kernel(faces_ref, send_ref, *held, *outs, lanes=lanes, tick=tick)


def prepare_kernel(
    star_ref, aminus_ref, aplus_ref, vol_ref, flux_ref, lift_ref, rotate_ref, neighbour_ref, orient_ref, send_ref,
    coef_out, aplus_out, left_out, lift_out, turn_out, near_out, far_out, send_out, *, lanes,
):
    half = lanes // 2
    pack_coefs(star_ref, 3, 0, coef_out)
    pack_coefs(aminus_ref, 4, 3, coef_out)
    for g in range(FIELDS):
        ahead, behind = star_ref[FIELDS - 1, g], aminus_ref[FIELDS - 1, g]
        pack_last([ahead[d : d + 1] for d in range(3)] + [behind[j : j + 1] for j in range(4)], g, coef_out)
        for f in range(FIELDS):
            own = aplus_ref[f, g]
            for k in range(2):
                aplus_out[f * FIELDS + g, k : k + 1, :] = pair(own[2 * k : 2 * k + 1], own[2 * k + 1 : 2 * k + 2])
    both = jnp.concatenate([vol_ref[...].reshape(3 * MODES, MODES), -flux_ref[...].reshape(4 * MODES, MODES)], axis=0)
    left_out[...] = left_parts(both, MODES_UP).astype(BF16)
    lift = jnp.concatenate([pad_rows(lift_ref[:, j, :], FACE_UP) for j in range(4)], axis=0)
    lift = jnp.concatenate([lift, jnp.zeros((4 * FACE_UP, lanes - MODES), F32)], axis=1)
    lift = jnp.transpose(pad_rows(lift, lanes))[0:MODES, 0 : 4 * FACE_UP]
    lift_out[...] = left_parts(lift, 4 * FACE_UP).astype(BF16)
    turns = jnp.concatenate([pad_rows(rotate_ref[which], FACE_UP) for which in range(3)], axis=0)
    turn_out[...] = jnp.concatenate([left_parts(turns, FACE_UP), jnp.zeros((3 * FACE_UP, SLOT), F32)], axis=1).astype(BF16)
    row = jnp.concatenate([neighbour_ref[j : j + 1, :] for j in range(4)], axis=1)
    turned = jnp.concatenate([orient_ref[j : j + 1, :] for j in range(4)], axis=1)
    near_out[...] = one_hot(row, 4 * half)
    sub = lax.broadcasted_iota(jnp.int32, (lanes, 4 * half), 0)
    for group in range(send_ref.shape[0]):
        target = 4 * half + ((sub // SLOT) % 4) * (4 * SLOT) + group * SLOT + sub % SLOT
        hit = (target == row) & (turned == sub // (4 * SLOT))
        far_out[group * lanes : (group + 1) * lanes, :] = jnp.where(hit, 1.0, 0.0).astype(BF16)
    for group in range(send_ref.shape[0]):
        send_out[:, group * lanes : (group + 1) * lanes] = send_hot(send_ref[group : group + 1, :], lanes)


def local_kernel(
    i_ref, packed_ref, faces_ref, cluster_ref, coef_ref, left_ref, near_ref, turn_ref, orient_ref, own_ref, seen_ref,
    send_ref, held_ref, base_out, own_out, seen_out, *rest, lanes, tick,
):
    m_ref, table_ref = rest[-2:]
    fill_table(faces_ref, table_ref, lanes)
    if tick < TICKS - 1:
        picked = pick_faces(faces_ref, send_ref[:, lanes:], lanes)
        rest[0][:, 0:lanes] = picked[:, 0:lanes]
        rest[0][:, lanes:] = held_ref[:, lanes:] + picked[:, lanes:] if tick else picked[:, lanes:]
    cluster = pair(cluster_ref[...], cluster_ref[...])
    offset, finished = timing(cluster, tick)
    two = jnp.concatenate([offset, offset], axis=1)
    for group in GROUPS:
        cols = span(group, lanes)
        values = i_ref[:, cols]
        if tick:
            fresh = (offset if len(group) == 1 else two) == 0
            values = jnp.where(fresh, values, own_ref[:, cols] + values)
        own_out[:, cols] = values
        products(m_ref, 0, left_ref[...], values, 7, group, lanes)
    seen = pick(table_ref[...], near_ref[...])
    which = jnp.concatenate([orient_ref[j : j + 1, :] for j in range(4)], axis=1)
    for f in range(FIELDS):
        rows = slice(f * FACE_UP, (f + 1) * FACE_UP)
        turned = jnp.dot(turn_ref[...], face_operand(seen[rows]), preferred_element_type=F32)
        part = jnp.where(
            which == 0,
            turned[0:FACE_UP],
            jnp.where(which == 1, turned[FACE_UP : 2 * FACE_UP], turned[2 * FACE_UP : 3 * FACE_UP]),
        )
        seen_out[rows, :] = jnp.where(two == 0, part, seen_ref[rows, :] + part) if tick else part
    seen_out[FIELDS * FACE_UP :, :] = jnp.zeros((ROWS - FIELDS * FACE_UP, 2 * lanes), F32)
    for group in GROUPS:
        cols = span(group, lanes)
        before = packed_ref[:, cols]
        change = contract(m_ref, 0, coef_ref, 7, group, lanes)
        done = finished if len(group) == 1 else jnp.concatenate([finished, finished], axis=1)
        base_out[:, cols] = jnp.where(done, before + change, before)


def update_kernel(
    r0, r1, r2, r3, near_ref, far_ref, turn_ref, aplus_ref, lift_ref, base_ref, cluster_ref, packed_ref, c_ref,
    *, lanes, tick, groups,
):
    _, finished = timing(pair(cluster_ref[...], cluster_ref[...]), tick)
    gather_faces((r0, r1, r2, r3), groups, near_ref, far_ref, turn_ref, aplus_ref, c_ref, lanes)
    for group in GROUPS:
        packed_ref[:, span(group, lanes)] = updated(c_ref, lift_ref, base_ref, finished, group, lanes)


def last_kernel(
    r0, r1, r2, r3, near_ref, far_ref, turn_ref, aplus_ref, lift_ref, base_ref, cluster_ref, result_hbm,
    c_ref, out_ref, gone, *, lanes,
):
    half = lanes // 2
    copies = []
    _, finished = timing(pair(cluster_ref[...], cluster_ref[...]), TICKS - 1)
    gather_faces((r0, r1, r2, r3), 4, near_ref, far_ref, turn_ref, aplus_ref, c_ref, lanes)
    for group in GROUPS:
        values = updated(c_ref, lift_ref, base_ref, finished, group, lanes)
        for i, q in enumerate(group):
            for side in range(2):
                if 2 * q + side < FIELDS:
                    out_ref[2 * q + side] = values[:, i * lanes + side * half : i * lanes + (side + 1) * half]
        fields = pl.ds(2 * group[0], min(2 * len(group), FIELDS - 2 * group[0]))
        copy = pltpu.make_async_copy(out_ref.at[fields], result_hbm.at[fields], gone.at[GROUPS.index(group)])
        copy.start()
        copies.append(copy)
    for copy in copies:
        copy.wait()


def stages(slots, dirs, lanes):
    wide = pltpu.VMEM((dirs * MODES, 2 * lanes), F32)
    last = pltpu.VMEM(((dirs + 1) // 2 * MODES, lanes), F32)
    return [[wide, wide, last] for _ in range(slots)]


def call(body, outs, scratch, name, flops, arrays, far=0, far_out=False):
    moved = sum(a.size * a.dtype.itemsize for a in arrays)
    hbm = pltpu.MemorySpace.HBM
    near = len(arrays) - far
    arrays = [*arrays[:near], *(pltpu.with_memory_space_constraint(x, hbm) for x in arrays[near:])]
    spaces = [pltpu.VMEM] * near + [hbm] * far
    return pl.pallas_call(
        body,
        out_shape=outs,
        in_specs=[pl.BlockSpec(memory_space=space) for space in spaces],
        out_specs=[pl.BlockSpec(memory_space=hbm if far_out else pltpu.VMEM)] * len(outs),
        scratch_shapes=scratch,
        compiler_params=pltpu.CompilerParams(vmem_limit_bytes=24 << 20),
        cost_estimate=pl.CostEstimate(flops=flops, bytes_accessed=moved, transcendentals=0),
        name=name,
    )(*arrays)


def shards(
    state, star, aminus, aplus, ck_stiff, vol_stiff, flux_local, lift, rotate, project,
    cluster, orient, neighbour, send_elem, send_face,
):
    elems = state.shape[-1]
    lanes = 2 * elems
    wide = PAIRS * lanes
    groups = send_elem.shape[1] // SLOT
    shape = jax.ShapeDtypeStruct
    cluster_row = cluster.reshape(1, elems)
    star, aminus, aplus = (jnp.transpose(x, (1, 2, 0, 3)) for x in (star, aminus, aplus))
    project = jnp.transpose(project, (1, 0, 2))
    lift = jnp.transpose(lift, (2, 0, 1))

    modal = shape((MODES, wide), F32)
    table = shape((ROWS, 4 * elems), F32)
    weights = pltpu.VMEM((SLOT, lanes), F32)
    faces = shape((4 * FACE_UP, wide), F32)
    staged = stages(2, 3, lanes)
    sides = pltpu.VMEM((12 * FACE_UP, wide), BF16)

    def like(x):
        return shape(x.shape, x.dtype)

    def room(x):
        return pltpu.VMEM(x.shape, x.dtype)

    def message(count):
        return [shape((count * FACE_UP, lanes), F32)] * 4

    late = (aminus, aplus, vol_stiff, flux_local, lift, rotate, neighbour, orient)
    packed, star_pairs, ck_left, proj_left, send, star, cluster_row, *late = call(
        functools.partial(first_kernel, lanes=lanes),
        [
            modal,
            shape((PAIRS * FIELDS, 3, lanes), F32),
            shape((3 * MODES, 3 * MODES_UP), BF16),
            shape((4 * FACE_UP, 3 * MODES_UP), BF16),
            shape((groups, lanes), jnp.int32),
            like(star),
            like(cluster_row),
        ]
        + [like(x) for x in late],
        [room(state), room(ck_stiff), room(project), room(send_elem), room(send_face)]
        + [pltpu.SemaphoreType.DMA((7,)), pltpu.SemaphoreType.DMA((len(late),))],
        "first", 10_000_000,
        (state, star, ck_stiff, project, cluster_row, send_elem, send_face, *late), far=7 + len(late),
    )
    orient = late[-1]

    def predicted(tick, packed, chosen, more):
        integral, face_values, *messages = call(
            functools.partial(predict_send_kernel, lanes=lanes, tick=tick),
            [modal, faces] + message(GROUPS_AT[tick]),
            [weights, staged],
            f"predict{tick}", 400_000_000,
            (packed, cluster_row, ck_left, star_pairs, proj_left, chosen, *more),
        )
        return integral, face_values, messages

    integral, face_values, messages = predicted(0, packed, send, ())
    coef, aplus_pairs, left, lift_left, turn, near_hot, far_hot, chosen = call(
        functools.partial(prepare_kernel, lanes=lanes),
        [
            shape((PAIRS * FIELDS, 7, lanes), F32),
            shape((FIELDS * FIELDS, 2, lanes), F32),
            shape((7 * MODES, 3 * MODES_UP), BF16),
            shape((MODES, 12 * FACE_UP), BF16),
            shape((3 * FACE_UP, 80), BF16),
            shape((4 * elems, 4 * elems), BF16),
            shape((groups * lanes, 4 * elems), BF16),
            shape((4 * lanes, groups * lanes), BF16),
        ],
        [],
        "prepare", 100_000_000,
        (star, *late, send),
    )
    own = integral
    seen = near_hot
    held = near_hot
    for tick in range(TICKS):
        arrived = [None] * 4
        for slot, axis, phase in ((1, "slab", 1), (0, "slab", 0), (3, "sub", 1), (2, "sub", 0)):
            arrived[slot] = exchange(messages[slot], axis, phase)
        last = tick == TICKS - 1
        base, own, seen, *kept = call(
            functools.partial(local_kernel, lanes=lanes, tick=tick),
            [modal, modal, table] + ([] if last else [shape((PAIRS * FACE_UP, (groups - 1) * lanes), F32)]),
            [stages(1, 7, lanes), pltpu.VMEM((ROWS, 4 * elems), F32)],
            f"local{tick}", 300_000_000,
            (integral, packed, face_values, cluster_row, coef, left, near_hot, turn, orient, own, seen, chosen, held),
        )
        held = held if last else kept[0]
        count = GROUPS_AT[tick]
        common = (*arrived, seen, far_hot, turn, aplus_pairs, lift_left, base, cluster_row)
        if last:
            return call(
                functools.partial(last_kernel, lanes=lanes),
                [shape(state.shape, F32)],
                [sides, room(state), pltpu.SemaphoreType.DMA((len(GROUPS),))],
                "last", 100_000_000, common, far_out=True,
            )[0]
        packed = call(
            functools.partial(update_kernel, lanes=lanes, tick=tick, groups=count),
            [modal],
            [sides],
            f"update{tick}", 100_000_000, common,
        )[0]
        integral, face_values, messages = predicted(tick + 1, packed, chosen, (held,) if tick % 2 == 0 else ())


def solution(mesh):
    placed = (
        P(None, None, ("slab", "sub")),
        P(None, None, None, ("slab", "sub")),
        P(None, None, None, ("slab", "sub")),
        P(None, None, None, ("slab", "sub")),
        P(),
        P(),
        P(),
        P(),
        P(),
        P(),
        P(("slab", "sub")),
        P(None, ("slab", "sub")),
        P(None, ("slab", "sub")),
        P(None, ("slab", "sub")),
        P(None, ("slab", "sub")),
    )
    return jax.shard_map(
        shards,
        mesh=mesh,
        in_specs=placed,
        out_specs=P(None, None, ("slab", "sub")),
        check_vma=False,
    )
```

```python
import functools

import jax
import jax.numpy as jnp
from jax import lax
from jax.experimental import pallas as pl
from jax.experimental.pallas import tpu as pltpu
from jax.sharding import PartitionSpec as P

FIELDS = 9
PAIRS = 5
MODES = 56
MODES_UP = 64
FACE_MODES = 21
FACE_UP = 24
ROWS = 2 * PAIRS * FACE_UP
DERIVS = 6
TICKS = 4
SLOT = 8
TIME_STEP = 1.0
F32 = jnp.float32
BF16 = jnp.bfloat16
BLOCKS = ((0, 32), (32, 24))
GROUPS = ((0, 1), (2, 3), (4,))
GROUPS_AT = (1, 2, 1, 4)


def paired(axis):
    return lax.axis_size(axis) % 2 == 0


def exchange(x, axis, phase):
    size = lax.axis_size(axis)
    if paired(axis):
        pairs = []
        for i in range(phase, size + phase, 2):
            one, two = i % size, (i + 1) % size
            pairs += [(one, two), (two, one)]
    else:
        by = 1 if phase == 0 else -1
        pairs = [(i, (i + by) % size) for i in range(size)]
    return lax.ppermute(x, axis, pairs)


def taylor_constants():
    width = TIME_STEP / TICKS
    table = []
    for begin in range(TICKS):
        factorial = 1.0
        row = []
        for order in range(DERIVS):
            factorial = factorial * (order + 1)
            span = float((begin + 1) ** (order + 1) - begin ** (order + 1))
            row.append(span * width ** (order + 1) / factorial)
        table.append(row)
    return table


def low_half(shape, half):
    return lax.broadcasted_iota(jnp.int32, shape, len(shape) - 1) < half


def swap(x, half):
    return pltpu.roll(x, half, x.ndim - 1)


def pair(a, b):
    return jnp.concatenate([a, b], axis=-1)


def halves(x):
    high = x.astype(BF16).astype(F32)
    return high, x - high


def pad_rows(x, rows):
    if x.shape[0] == rows:
        return x
    return jnp.concatenate([x, jnp.zeros((rows - x.shape[0], x.shape[1]), x.dtype)], axis=0)


def timing(cluster, tick):
    period = jnp.where(cluster == 0, 4, jnp.where(cluster == 1, 2, 1))
    offset = jnp.where(cluster == 0, tick % 4, jnp.where(cluster == 1, tick % 2, 0))
    return offset, offset == period - 1


def right_operand(values):
    values = pad_rows(values, MODES_UP)
    high = values.astype(BF16)
    low = (values - high.astype(F32)).astype(BF16)
    return jnp.concatenate([high, high, low], axis=0)


def left_parts(matrix, up):
    rows = matrix.shape[0]
    if up > matrix.shape[1]:
        matrix = jnp.concatenate([matrix, jnp.zeros((rows, up - matrix.shape[1]), F32)], axis=1)
    high, low = halves(matrix)
    return jnp.concatenate([high, low, high], axis=1)


def send_choice(even, forward, backward):
    return jnp.where(even, forward, backward), jnp.where(even, backward, forward)


def parity(axis):
    if not paired(axis):
        return True, False
    even = lax.rem(lax.axis_index(axis), 2) == 0
    return even, even


def products(m_ref, slot, left, values, dirs, group, lanes):
    out = jnp.dot(left, right_operand(values), preferred_element_type=F32)
    if group == GROUPS[-1]:
        low = low_half((MODES, lanes), lanes // 2)
        for i in range(0, dirs, 2):
            one = out[i * MODES : (i + 1) * MODES]
            if i + 1 < dirs:
                one = jnp.where(low, one, out[(i + 1) * MODES : (i + 2) * MODES])
            m_ref[slot][-1][(i // 2) * MODES : (i // 2 + 1) * MODES, :] = one
    else:
        m_ref[slot][GROUPS.index(group)][...] = out


def contract(m_ref, slot, coef_ref, dirs, group, lanes):
    half = lanes // 2
    fields = [g for q in group for g in (2 * q, 2 * q + 1) if g < FIELDS]
    terms = [(d, q, q, d) for q in range(PAIRS - 1) for d in range(dirs)]
    terms += [(i, PAIRS - 1, PAIRS - 1, i) for i in range((dirs + 1) // 2)]
    columns = {q: [] for q in group}
    for row, count in BLOCKS:
        sums = {}
        for d, q, block, line in terms:
            at = (q % 2) * lanes
            values = m_ref[slot][q // 2][d * MODES + row : d * MODES + row + count, at : at + lanes]
            for g in fields:
                term = coef_ref[block * FIELDS + g, line : line + 1, :] * values
                sums[g] = sums[g] + term if g in sums else term
        low = low_half((count, lanes), half)
        for q in group:
            first = sums[2 * q]
            if 2 * q + 1 < FIELDS:
                second = sums[2 * q + 1]
                result = jnp.where(low, first, second) + swap(jnp.where(low, second, first), half)
            else:
                result = first + swap(first, half)
            columns[q].append(result)
    columns = [jnp.concatenate(columns[q], axis=0) for q in group]
    return columns[0] if len(columns) == 1 else jnp.concatenate(columns, axis=1)


def span(group, lanes):
    return slice(group[0] * lanes, (group[-1] + 1) * lanes)


def predict(state_of, ck_ref, star_ref, weight_ref, proj_ref, face_ref, m_ref, i_ref, lanes):
    def weight(order, group):
        row = weight_ref[order : order + 1, :]
        return row if len(group) == 1 else pair(row, row)

    for group in GROUPS:
        values = state_of(group)
        i_ref[:, span(group, lanes)] = weight(0, group) * values
        products(m_ref, 0, ck_ref[...], values, 3, group, lanes)
    for order in range(1, DERIVS):
        for group in GROUPS:
            values = contract(m_ref, (order - 1) % 2, star_ref, 3, group, lanes)
            total = i_ref[:, span(group, lanes)] + weight(order, group) * values
            i_ref[:, span(group, lanes)] = total
            if order < DERIVS - 1:
                products(m_ref, order % 2, ck_ref[...], values, 3, group, lanes)
            else:
                face_ref[:, span(group, lanes)] = jnp.dot(
                    proj_ref[...], right_operand(total), preferred_element_type=F32
                )


def store_weights(weight_ref, cluster, tick):
    offset, _ = timing(cluster, tick)
    table = taylor_constants()
    for order in range(DERIVS):
        row = jnp.full(cluster.shape, table[0][order], F32)
        for begin in range(1, TICKS):
            row = jnp.where(offset == begin, table[begin][order], row)
        weight_ref[order : order + 1, :] = row


def fill_table(face_ref, table_ref, lanes):
    half = lanes // 2
    low = low_half((FACE_UP, lanes), half)
    for q in range(PAIRS):
        for k in range(2):
            one = face_ref[2 * k * FACE_UP : (2 * k + 1) * FACE_UP, q * lanes : (q + 1) * lanes]
            two = face_ref[(2 * k + 1) * FACE_UP : (2 * k + 2) * FACE_UP, q * lanes : (q + 1) * lanes]
            crossed = swap(jnp.where(low, two, one), half)
            table_ref[2 * q * FACE_UP : (2 * q + 1) * FACE_UP, k * lanes : (k + 1) * lanes] = jnp.where(low, one, crossed)
            table_ref[(2 * q + 1) * FACE_UP : (2 * q + 2) * FACE_UP, k * lanes : (k + 1) * lanes] = jnp.where(
                low, crossed, two
            )


def pick(table, chosen):
    rows = table.shape[0]
    high, low = halves(table)
    both = jnp.concatenate([high, low], axis=0).astype(BF16)
    out = jnp.dot(both, chosen, preferred_element_type=F32)
    return out[:rows] + out[rows:]


def one_hot(index_row, rows):
    sub = lax.broadcasted_iota(jnp.int32, (rows, index_row.shape[1]), 0)
    return jnp.where(sub == index_row, 1.0, 0.0).astype(BF16)


def send_hot(index_row, lanes):
    half = lanes // 2
    column, _ = lane_places(1, lanes)
    sub = lax.broadcasted_iota(jnp.int32, (half, lanes), 0)
    blocks = []
    for j in range(4):
        for side in range(2):
            target = jnp.where(column % 2 == side, index_row - j * half, -1)
            blocks.append(jnp.where(sub == target, 1.0, 0.0).astype(BF16))
    return jnp.concatenate(blocks, axis=0)


def pick_faces(face_ref, chosen, lanes):
    rows = []
    for q in range(PAIRS):
        cols = slice(q * lanes, (q + 1) * lanes)
        rows.append(jnp.concatenate([face_ref[j * FACE_UP : (j + 1) * FACE_UP, cols] for j in range(4)], axis=1))
    return pick(jnp.concatenate(rows, axis=0), chosen)


def lane_places(rows, lanes):
    lane = lax.broadcasted_iota(jnp.int32, (rows, lanes), 1)
    return lane // (4 * SLOT), (lane // SLOT) % 4


def send_rows(face_ref, elem_ref, lanes):
    slots = face_ref.shape[1]
    half = lanes // 2
    index = face_ref[...] * half + elem_ref[...]
    index = jnp.concatenate([index] * (lanes // slots), axis=1)
    _, place = lane_places(1, lanes)
    rows = []
    for group in range(slots // SLOT):
        row = None
        for d in range(4):
            shift = ((d - group) * SLOT) % lanes
            moved = index[d : d + 1, :]
            moved = pltpu.roll(moved, shift, 1) if shift else moved
            row = moved if row is None else jnp.where(place == d, moved, row)
        rows.append(row)
    return rows


def fill_messages(picks, out_refs, lanes):
    column, place = lane_places(FACE_UP, lanes)
    for group, picked in enumerate(picks):
        pairs = [picked[q * FACE_UP : (q + 1) * FACE_UP] for q in range(PAIRS)]
        quads = [jnp.where(column < 2, pairs[0], pairs[1]), jnp.where(column < 2, pairs[2], pairs[3]), pairs[4]]
        messages = []
        for d in range(4):
            message = None
            for quad in range(3):
                shift = ((quad - d) * SLOT) % lanes
                moved = quads[quad] if shift == 0 else pltpu.roll(quads[quad], shift, 1)
                message = moved if message is None else jnp.where(place == quad, moved, message)
            messages.append(message)
        for axis, first in (("slab", 0), ("sub", 2)):
            even, _ = parity(axis)
            one, two = send_choice(even, messages[first], messages[first + 1])
            out_refs[first][group * FACE_UP : (group + 1) * FACE_UP, :] = one
            out_refs[first + 1][group * FACE_UP : (group + 1) * FACE_UP, :] = two


def face_operand(values):
    high, low = halves(values)
    return jnp.concatenate([high, high, low, jnp.zeros((SLOT, values.shape[1]), F32)], axis=0).astype(BF16)


def take_messages(in_refs, groups, far_ref, turn_ref, lanes):
    column, place = lane_places(FACE_UP, lanes)
    quads = []
    for group in range(groups):
        arrived = [ref[group * FACE_UP : (group + 1) * FACE_UP, :] for ref in in_refs]
        for axis, first in (("slab", 0), ("sub", 2)):
            _, even = parity(axis)
            arrived[first], arrived[first + 1] = send_choice(even, arrived[first + 1], arrived[first])
        for quad in range(3):
            merged = None
            for d in range(4):
                shift = ((d - quad) * SLOT) % lanes
                moved = arrived[d] if shift == 0 else pltpu.roll(arrived[d], shift, 1)
                merged = moved if merged is None else jnp.where(place == d, moved, merged)
            quads.append(merged)
    turned = jnp.dot(turn_ref[...], face_operand(jnp.concatenate(quads, axis=1)), preferred_element_type=F32)
    columns = []
    for group in range(groups):
        pieces = []
        for quad in range(3):
            at = (3 * group + quad) * lanes
            sides = [turned[which * FACE_UP : (which + 1) * FACE_UP, at : at + lanes] for which in range(3)]
            count = min(4, FIELDS - 4 * quad)
            moved = []
            for by in range(4 if count > 1 else 3):
                if count > 1:
                    source = sides[2]
                    for which in range(2):
                        source = jnp.where(column == (which - by) % 4, sides[which], source)
                else:
                    source = sides[by]
                moved.append(pltpu.roll(source, by * 4 * SLOT, 1) if by else source)
            for c in range(count):
                piece = moved[(2 - c) % 4]
                for which in range(2):
                    piece = jnp.where(column == which, moved[(which - c) % 4], piece)
                pieces.append(piece)
        columns.append(jnp.concatenate(pieces, axis=0))
    left = columns[0] if groups == 1 else jnp.concatenate(columns, axis=1)
    chosen = far_ref[0 : groups * lanes, :]
    if groups > 1:
        return pick(left, chosen)
    high, low = halves(left)
    both = jnp.concatenate([high, low], axis=1).astype(BF16)
    return jnp.dot(both, jnp.concatenate([chosen, chosen], axis=0), preferred_element_type=F32)


def gather_faces(in_refs, groups, near_ref, far_ref, turn_ref, aplus_ref, c_ref, lanes):
    half = lanes // 2
    low = low_half((FACE_UP, lanes), half)
    values = near_ref[0 : FIELDS * FACE_UP, :] + take_messages(in_refs, groups, far_ref, turn_ref, lanes)
    for group in GROUPS:
        fields = [g for q in group for g in (2 * q, 2 * q + 1) if g < FIELDS]
        for k in range(2):
            sums = {}
            for f in range(FIELDS):
                part = values[f * FACE_UP : (f + 1) * FACE_UP, k * lanes : (k + 1) * lanes]
                for g in fields:
                    term = aplus_ref[f * FIELDS + g, k : k + 1, :] * part
                    sums[g] = sums[g] + term if g in sums else term
            for q in group:
                first = sums[2 * q]
                second = sums[min(2 * q + 1, FIELDS - 1)]
                crossed = swap(jnp.where(low, second, first), half)
                sides = jnp.concatenate([jnp.where(low, first, crossed), jnp.where(low, crossed, second)], axis=0)
                high = sides.astype(BF16)
                rest = (sides - high.astype(F32)).astype(BF16)
                at, cols = 2 * k * FACE_UP, slice(q * lanes, (q + 1) * lanes)
                c_ref[at : at + 2 * FACE_UP, cols] = high
                c_ref[4 * FACE_UP + at : 4 * FACE_UP + at + 2 * FACE_UP, cols] = high
                c_ref[8 * FACE_UP + at : 8 * FACE_UP + at + 2 * FACE_UP, cols] = rest


def updated(c_ref, lift_ref, base_ref, finished, group, lanes):
    cols = span(group, lanes)
    outer = jnp.dot(lift_ref[...], c_ref[:, cols], preferred_element_type=F32)
    before = base_ref[:, cols]
    done = finished if len(group) == 1 else jnp.concatenate([finished, finished], axis=1)
    return jnp.where(done, before - outer, before)


def pack_coefs(ref, dirs, base, out_ref):
    for q in range(PAIRS - 1):
        for g in range(FIELDS):
            out_ref[q * FIELDS + g, base : base + dirs, :] = pair(ref[2 * q, g], ref[2 * q + 1, g])


def pack_last(lines, g, out_ref):
    for i in range(0, len(lines), 2):
        other = lines[i + 1] if i + 1 < len(lines) else jnp.zeros_like(lines[i])
        out_ref[(PAIRS - 1) * FIELDS + g, i // 2 : i // 2 + 1, :] = pair(lines[i], other)


def first_kernel(
    state_hbm, star_hbm, ck_hbm, project_hbm, cluster_hbm, elem_hbm, face_hbm, *rest, lanes
):
    count = (len(rest) - 14) // 2
    late_hbm, rest = rest[:count], rest[count:]
    packed_ref, star_out, ck_out, proj_out, send_out, star_ref, cluster_ref = rest[:7]
    late_out, rest = rest[7 : 7 + count], rest[7 + count :]
    state_ref, ck_ref, project_ref, elem_ref, face_ref, early, late = rest
    soon = [
        pltpu.make_async_copy(source, target, early.at[i])
        for i, (source, target) in enumerate((
            (star_hbm, star_ref), (state_hbm, state_ref), (ck_hbm, ck_ref), (project_hbm, project_ref),
            (elem_hbm, elem_ref), (face_hbm, face_ref), (cluster_hbm, cluster_ref),
        ))
    ]
    then = [pltpu.make_async_copy(a, b, late.at[i]) for i, (a, b) in enumerate(zip(late_hbm, late_out))]
    for copy in soon + then:
        copy.start()
    soon[0].wait()
    pack_coefs(star_ref, 3, 0, star_out)
    for g in range(FIELDS):
        both = star_ref[FIELDS - 1, g]
        pack_last([both[d : d + 1] for d in range(3)], g, star_out)
    soon[1].wait()
    for q in range(PAIRS):
        packed_ref[:, q * lanes : (q + 1) * lanes] = pair(state_ref[2 * q], state_ref[min(2 * q + 1, FIELDS - 1)])
    for copy in soon[2:]:
        copy.wait()
    ck_out[...] = left_parts(-ck_ref[...].reshape(3 * MODES, MODES), MODES_UP).astype(BF16)
    proj_rows = [pad_rows(project_ref[:, j, :], FACE_UP) for j in range(4)]
    proj_out[...] = left_parts(jnp.concatenate(proj_rows, axis=0), MODES_UP).astype(BF16)
    for i, row in enumerate(send_rows(face_ref, elem_ref, lanes)):
        send_out[i : i + 1, :] = row
    for copy in then:
        copy.wait()


def predict_kernel(
    packed_ref, cluster_ref, ck_ref, star_ref, proj_ref, i_ref, faces_ref, weight_ref, m_ref, *, lanes, tick
):
    store_weights(weight_ref, pair(cluster_ref[...], cluster_ref[...]), tick)

    def state_of(group):
        return packed_ref[:, span(group, lanes)]

    predict(state_of, ck_ref, star_ref, weight_ref, proj_ref, faces_ref, m_ref, i_ref, lanes)


def send_kernel(faces_ref, send_ref, *rest, lanes, tick):
    if tick % 2:
        held_ref, rest = rest[0], rest[1:]
    count = GROUPS_AT[tick]
    chosen = send_ref[:, 0 : count * lanes] if tick else send_hot(send_ref[0:1, :], lanes)
    picked = pick_faces(faces_ref, chosen, lanes)
    picks = [picked[:, group * lanes : (group + 1) * lanes] for group in range(count)]
    for group in range(1, count):
        picks[group] = picks[group] + held_ref[:, (group - 1) * lanes : group * lanes]
    fill_messages(picks, rest, lanes)


def predict_send_kernel(packed_ref, cluster_ref, ck_ref, star_ref, proj_ref, send_ref, *rest, lanes, tick):
    held = rest[:1] if tick % 2 else ()
    i_ref, faces_ref, *outs = rest[len(held) : len(held) + 6]
    weight_ref, m_ref = rest[len(held) + 6 :]
    predict_kernel(
        packed_ref, cluster_ref, ck_ref, star_ref, proj_ref, i_ref, faces_ref, weight_ref, m_ref, lanes=lanes, tick=tick
    )
    send_kernel(faces_ref, send_ref, *held, *outs, lanes=lanes, tick=tick)


def prepare_kernel(
    star_ref, aminus_ref, aplus_ref, vol_ref, flux_ref, lift_ref, rotate_ref, neighbour_ref, orient_ref, send_ref,
    coef_out, aplus_out, left_out, lift_out, turn_out, near_out, far_out, send_out, *, lanes,
):
    half = lanes // 2
    pack_coefs(star_ref, 3, 0, coef_out)
    pack_coefs(aminus_ref, 4, 3, coef_out)
    for g in range(FIELDS):
        ahead, behind = star_ref[FIELDS - 1, g], aminus_ref[FIELDS - 1, g]
        pack_last([ahead[d : d + 1] for d in range(3)] + [behind[j : j + 1] for j in range(4)], g, coef_out)
        for f in range(FIELDS):
            own = aplus_ref[f, g]
            for k in range(2):
                aplus_out[f * FIELDS + g, k : k + 1, :] = pair(own[2 * k : 2 * k + 1], own[2 * k + 1 : 2 * k + 2])
    both = jnp.concatenate([vol_ref[...].reshape(3 * MODES, MODES), -flux_ref[...].reshape(4 * MODES, MODES)], axis=0)
    left_out[...] = left_parts(both, MODES_UP).astype(BF16)
    lift = jnp.concatenate([pad_rows(lift_ref[:, j, :], FACE_UP) for j in range(4)], axis=0)
    lift = jnp.concatenate([lift, jnp.zeros((4 * FACE_UP, lanes - MODES), F32)], axis=1)
    lift = jnp.transpose(pad_rows(lift, lanes))[0:MODES, 0 : 4 * FACE_UP]
    lift_out[...] = left_parts(lift, 4 * FACE_UP).astype(BF16)
    turns = jnp.concatenate([pad_rows(rotate_ref[which], FACE_UP) for which in range(3)], axis=0)
    turn_out[...] = jnp.concatenate([left_parts(turns, FACE_UP), jnp.zeros((3 * FACE_UP, SLOT), F32)], axis=1).astype(BF16)
    row = jnp.concatenate([neighbour_ref[j : j + 1, :] for j in range(4)], axis=1)
    turned = jnp.concatenate([orient_ref[j : j + 1, :] for j in range(4)], axis=1)
    near_out[...] = one_hot(row, 4 * half)
    sub = lax.broadcasted_iota(jnp.int32, (lanes, 4 * half), 0)
    for group in range(send_ref.shape[0]):
        target = 4 * half + ((sub // SLOT) % 4) * (4 * SLOT) + group * SLOT + sub % SLOT
        hit = (target == row) & (turned == sub // (4 * SLOT))
        far_out[group * lanes : (group + 1) * lanes, :] = jnp.where(hit, 1.0, 0.0).astype(BF16)
    for group in range(send_ref.shape[0]):
        send_out[:, group * lanes : (group + 1) * lanes] = send_hot(send_ref[group : group + 1, :], lanes)


def local_kernel(
    i_ref, packed_ref, faces_ref, cluster_ref, coef_ref, left_ref, near_ref, turn_ref, orient_ref, own_ref, seen_ref,
    send_ref, held_ref, base_out, own_out, seen_out, *rest, lanes, tick,
):
    m_ref, table_ref = rest[-2:]
    fill_table(faces_ref, table_ref, lanes)
    if tick < TICKS - 1:
        picked = pick_faces(faces_ref, send_ref[:, lanes:], lanes)
        rest[0][:, 0:lanes] = picked[:, 0:lanes]
        rest[0][:, lanes:] = held_ref[:, lanes:] + picked[:, lanes:] if tick else picked[:, lanes:]
    cluster = pair(cluster_ref[...], cluster_ref[...])
    offset, finished = timing(cluster, tick)
    two = jnp.concatenate([offset, offset], axis=1)
    for group in GROUPS:
        cols = span(group, lanes)
        values = i_ref[:, cols]
        if tick:
            fresh = (offset if len(group) == 1 else two) == 0
            values = jnp.where(fresh, values, own_ref[:, cols] + values)
        own_out[:, cols] = values
        products(m_ref, 0, left_ref[...], values, 7, group, lanes)
    seen = pick(table_ref[...], near_ref[...])
    which = jnp.concatenate([orient_ref[j : j + 1, :] for j in range(4)], axis=1)
    for f in range(FIELDS):
        rows = slice(f * FACE_UP, (f + 1) * FACE_UP)
        turned = jnp.dot(turn_ref[...], face_operand(seen[rows]), preferred_element_type=F32)
        part = jnp.where(
            which == 0,
            turned[0:FACE_UP],
            jnp.where(which == 1, turned[FACE_UP : 2 * FACE_UP], turned[2 * FACE_UP : 3 * FACE_UP]),
        )
        seen_out[rows, :] = jnp.where(two == 0, part, seen_ref[rows, :] + part) if tick else part
    seen_out[FIELDS * FACE_UP :, :] = jnp.zeros((ROWS - FIELDS * FACE_UP, 2 * lanes), F32)
    for group in GROUPS:
        cols = span(group, lanes)
        before = packed_ref[:, cols]
        change = contract(m_ref, 0, coef_ref, 7, group, lanes)
        done = finished if len(group) == 1 else jnp.concatenate([finished, finished], axis=1)
        base_out[:, cols] = jnp.where(done, before + change, before)


def update_kernel(
    r0, r1, r2, r3, near_ref, far_ref, turn_ref, aplus_ref, lift_ref, base_ref, cluster_ref, packed_ref, c_ref,
    *, lanes, tick, groups,
):
    _, finished = timing(pair(cluster_ref[...], cluster_ref[...]), tick)
    gather_faces((r0, r1, r2, r3), groups, near_ref, far_ref, turn_ref, aplus_ref, c_ref, lanes)
    for group in GROUPS:
        packed_ref[:, span(group, lanes)] = updated(c_ref, lift_ref, base_ref, finished, group, lanes)


def last_kernel(
    r0, r1, r2, r3, near_ref, far_ref, turn_ref, aplus_ref, lift_ref, base_ref, cluster_ref, result_hbm,
    c_ref, out_ref, gone, *, lanes,
):
    half = lanes // 2
    copies = []
    _, finished = timing(pair(cluster_ref[...], cluster_ref[...]), TICKS - 1)
    gather_faces((r0, r1, r2, r3), 4, near_ref, far_ref, turn_ref, aplus_ref, c_ref, lanes)
    for group in GROUPS:
        values = updated(c_ref, lift_ref, base_ref, finished, group, lanes)
        for i, q in enumerate(group):
            for side in range(2):
                if 2 * q + side < FIELDS:
                    out_ref[2 * q + side] = values[:, i * lanes + side * half : i * lanes + (side + 1) * half]
        fields = pl.ds(2 * group[0], min(2 * len(group), FIELDS - 2 * group[0]))
        copy = pltpu.make_async_copy(out_ref.at[fields], result_hbm.at[fields], gone.at[GROUPS.index(group)])
        copy.start()
        copies.append(copy)
    for copy in copies:
        copy.wait()


def stages(slots, dirs, lanes):
    wide = pltpu.VMEM((dirs * MODES, 2 * lanes), F32)
    last = pltpu.VMEM(((dirs + 1) // 2 * MODES, lanes), F32)
    return [[wide, wide, last] for _ in range(slots)]


def call(body, outs, scratch, name, flops, arrays, far=0, far_out=False):
    moved = sum(a.size * a.dtype.itemsize for a in arrays)
    hbm = pltpu.MemorySpace.HBM
    near = len(arrays) - far
    arrays = [*arrays[:near], *(pltpu.with_memory_space_constraint(x, hbm) for x in arrays[near:])]
    spaces = [pltpu.VMEM] * near + [hbm] * far
    return pl.pallas_call(
        body,
        out_shape=outs,
        in_specs=[pl.BlockSpec(memory_space=space) for space in spaces],
        out_specs=[pl.BlockSpec(memory_space=hbm if far_out else pltpu.VMEM)] * len(outs),
        scratch_shapes=scratch,
        compiler_params=pltpu.CompilerParams(vmem_limit_bytes=24 << 20),
        cost_estimate=pl.CostEstimate(flops=flops, bytes_accessed=moved, transcendentals=0),
        name=name,
    )(*arrays)


def shards(
    state, star, aminus, aplus, ck_stiff, vol_stiff, flux_local, lift, rotate, project,
    cluster, orient, neighbour, send_elem, send_face,
):
    elems = state.shape[-1]
    lanes = 2 * elems
    wide = PAIRS * lanes
    groups = send_elem.shape[1] // SLOT
    shape = jax.ShapeDtypeStruct
    cluster_row = cluster.reshape(1, elems)
    star, aminus, aplus = (jnp.transpose(x, (1, 2, 0, 3)) for x in (star, aminus, aplus))
    project = jnp.transpose(project, (1, 0, 2))
    lift = jnp.transpose(lift, (2, 0, 1))

    modal = shape((MODES, wide), F32)
    table = shape((ROWS, 4 * elems), F32)
    weights = pltpu.VMEM((SLOT, lanes), F32)
    faces = shape((4 * FACE_UP, wide), F32)
    staged = stages(2, 3, lanes)
    sides = pltpu.VMEM((12 * FACE_UP, wide), BF16)

    def like(x):
        return shape(x.shape, x.dtype)

    def room(x):
        return pltpu.VMEM(x.shape, x.dtype)

    def message(count):
        return [shape((count * FACE_UP, lanes), F32)] * 4

    late = (aminus, aplus, vol_stiff, flux_local, lift, rotate, neighbour, orient)
    packed, star_pairs, ck_left, proj_left, send, star, cluster_row, *late = call(
        functools.partial(first_kernel, lanes=lanes),
        [
            modal,
            shape((PAIRS * FIELDS, 3, lanes), F32),
            shape((3 * MODES, 3 * MODES_UP), BF16),
            shape((4 * FACE_UP, 3 * MODES_UP), BF16),
            shape((groups, lanes), jnp.int32),
            like(star),
            like(cluster_row),
        ]
        + [like(x) for x in late],
        [room(state), room(ck_stiff), room(project), room(send_elem), room(send_face)]
        + [pltpu.SemaphoreType.DMA((7,)), pltpu.SemaphoreType.DMA((len(late),))],
        "first", 10_000_000,
        (state, star, ck_stiff, project, cluster_row, send_elem, send_face, *late), far=7 + len(late),
    )
    orient = late[-1]

    def predicted(tick, packed, chosen, more):
        integral, face_values, *messages = call(
            functools.partial(predict_send_kernel, lanes=lanes, tick=tick),
            [modal, faces] + message(GROUPS_AT[tick]),
            [weights, staged],
            f"predict{tick}", 400_000_000,
            (packed, cluster_row, ck_left, star_pairs, proj_left, chosen, *more),
        )
        return integral, face_values, messages

    integral, face_values, messages = predicted(0, packed, send, ())
    coef, aplus_pairs, left, lift_left, turn, near_hot, far_hot, chosen = call(
        functools.partial(prepare_kernel, lanes=lanes),
        [
            shape((PAIRS * FIELDS, 7, lanes), F32),
            shape((FIELDS * FIELDS, 2, lanes), F32),
            shape((7 * MODES, 3 * MODES_UP), BF16),
            shape((MODES, 12 * FACE_UP), BF16),
            shape((3 * FACE_UP, 80), BF16),
            shape((4 * elems, 4 * elems), BF16),
            shape((groups * lanes, 4 * elems), BF16),
            shape((4 * lanes, groups * lanes), BF16),
        ],
        [],
        "prepare", 100_000_000,
        (star, *late, send),
    )
    own = integral
    seen = near_hot
    held = near_hot
    for tick in range(TICKS):
        arrived = [None] * 4
        for slot, axis, phase in ((1, "slab", 1), (0, "slab", 0), (3, "sub", 1), (2, "sub", 0)):
            arrived[slot] = exchange(messages[slot], axis, phase)
        last = tick == TICKS - 1
        base, own, seen, *kept = call(
            functools.partial(local_kernel, lanes=lanes, tick=tick),
            [modal, modal, table] + ([] if last else [shape((PAIRS * FACE_UP, (groups - 1) * lanes), F32)]),
            [stages(1, 7, lanes), pltpu.VMEM((ROWS, 4 * elems), F32)],
            f"local{tick}", 300_000_000,
            (integral, packed, face_values, cluster_row, coef, left, near_hot, turn, orient, own, seen, chosen, held),
        )
        held = held if last else kept[0]
        count = GROUPS_AT[tick]
        common = (*arrived, seen, far_hot, turn, aplus_pairs, lift_left, base, cluster_row)
        if last:
            return call(
                functools.partial(last_kernel, lanes=lanes),
                [shape(state.shape, F32)],
                [sides, room(state), pltpu.SemaphoreType.DMA((len(GROUPS),))],
                "last", 100_000_000, common, far_out=True,
            )[0]
        packed = call(
            functools.partial(update_kernel, lanes=lanes, tick=tick, groups=count),
            [modal],
            [sides],
            f"update{tick}", 100_000_000, common,
        )[0]
        integral, face_values, messages = predicted(tick + 1, packed, chosen, (held,) if tick % 2 == 0 else ())


def solution(mesh):
    placed = (
        P(None, None, ("slab", "sub")),
        P(None, None, None, ("slab", "sub")),
        P(None, None, None, ("slab", "sub")),
        P(None, None, None, ("slab", "sub")),
        P(),
        P(),
        P(),
        P(),
        P(),
        P(),
        P(("slab", "sub")),
        P(None, ("slab", "sub")),
        P(None, ("slab", "sub")),
        P(None, ("slab", "sub")),
        P(None, ("slab", "sub")),
    )
    return jax.shard_map(
        shards,
        mesh=mesh,
        in_specs=placed,
        out_specs=P(None, None, ("slab", "sub")),
        check_vma=False,
    )
```
